256 devices in a mesh: row: 8 (over z), col: 32 (over y, x, core).
Axes of the slice: x: 4, y: 4, z: 8, core: 2. Of those that a mesh axis runs over, the one named last changes fastest.
Arguments:
- point_data: float32 [4, 65536], P(None, ('row', 'col')), may hold values from 0 to 32, as said below
- right_side: float32 [64, 65536], P(None, ('row', 'col')), may hold values from -45 to 45
- pair_list: int32 [2, 4444], replicated, may hold values from 0 to 511, as said below
Outputs:
- solution: float32 [64, 65536], P(None, ('row', 'col'))
- residual: float32 [64, 65536], P(None, ('row', 'col'))
The draws below stay inside these ranges and needn't reach their ends.
Inputs may be any that keep to these rules, and one draw needn't show every extreme that they name: `point_data`: the points of block b lie in one unit cell of a 4 x 4 x 32 grid, one block to a cell; row 3 lies in 0.2 to 0.6. `pair_list`: each column (I, J) has I < J and names two blocks whose cells lie within one cell of each other along every dimension; every such pair is listed exactly once. The columns stand grouped by the device (I // 2 // 32, (J // 2) % 32) of the row and col axes, groups in row-major order.
All inputs are finite; a program needn't handle non-finite values.
Results may differ from the reference program's by a relative error of at most 0.018.
Values may be sent and summed in bfloat16 or wider, within the bound.
A program may use at most 64 MiB of HBM per device.

```python
import math
import jax
import jax.numpy as jnp
import numpy as np
from jax import lax

BLOCK = 128
COLS = 64
ITERS = 3
SIDE = 4
BLK_DEV = 2
COL_DEVS = 32
NB = 512
N = 65536
DEPTH = 32


def block_layout(key):
    return jax.random.permutation(jax.random.fold_in(key, 11), NB)


def neighbour_cells():
    index = np.arange(SIDE * SIDE * DEPTH)
    along_x = index // (SIDE * DEPTH)
    along_y = index // DEPTH % SIDE
    along_z = index % DEPTH
    lower_cells = []
    upper_cells = []
    for shift_x in (-1, 0, 1):
        for shift_y in (-1, 0, 1):
            for shift_z in (-1, 0, 1):
                moved_x = along_x + shift_x
                moved_y = along_y + shift_y
                moved_z = along_z + shift_z
                inside = (moved_x >= 0) & (moved_x < SIDE) & (moved_y >= 0) & (moved_y < SIDE) & (moved_z >= 0) & (moved_z < DEPTH)
                target = (moved_x * SIDE + moved_y) * DEPTH + moved_z
                keep = inside & (target > index)
                lower_cells.append(index[keep])
                upper_cells.append(target[keep])
    return (np.concatenate(lower_cells), np.concatenate(upper_cells))


def draw_pair_list(key, part):
    layout = block_layout(key)
    block_of_cell = jnp.argsort(layout)
    lower_cells, upper_cells = neighbour_cells()
    one_block = block_of_cell[jnp.asarray(lower_cells, jnp.int32)]
    other_block = block_of_cell[jnp.asarray(upper_cells, jnp.int32)]
    low_block = jnp.minimum(one_block, other_block)
    high_block = jnp.maximum(one_block, other_block)
    device_of = low_block // BLK_DEV // COL_DEVS * COL_DEVS + high_block // BLK_DEV % COL_DEVS
    ordering = jnp.argsort(device_of * NB + low_block, stable=True)
    return jnp.stack([low_block[ordering], high_block[ordering]]).astype(jnp.int32)


def draw_point_data(key, part):
    layout = block_layout(key)
    cell_x = layout // (SIDE * DEPTH)
    cell_y = layout // DEPTH % SIDE
    cell_z = layout % DEPTH
    corner = jnp.stack([cell_x, cell_y, cell_z]).astype(jnp.float32)
    inner_key, scale_key = jax.random.split(jax.random.fold_in(key, 23))
    uniform = jax.random.uniform(inner_key, (3, NB, BLOCK), jnp.float32)
    inside = uniform
    scales = jnp.exp(jax.random.uniform(scale_key, (NB, BLOCK), jnp.float32, math.log(0.2), math.log(0.6)))
    coords = corner[:, :, None] + inside
    return jnp.concatenate([coords, scales[None]], axis=0).reshape(4, NB * BLOCK).astype(jnp.float32)


def draw_right_side(key, part):
    base_key, row_key, column_key = jax.random.split(jax.random.fold_in(key, 31), 3)
    position = jnp.arange(N).astype(jnp.float32) / N
    trend = 0.5 + position
    row_scale = jnp.exp(jax.random.uniform(row_key, (N,), jnp.float32, math.log(0.3), math.log(3.0)))
    column_scale = jnp.exp(jax.random.uniform(column_key, (COLS,), jnp.float32, math.log(0.5), math.log(2.0)))
    base = jnp.clip(jax.random.normal(base_key, (COLS, N), jnp.float32), -5.0, 5.0)
    return (base * (row_scale * trend)[None, :] * column_scale[:, None]).astype(jnp.float32)


def setup_inputs(seed: int = 0) -> dict:
    arg_keys = jax.random.split(jax.random.key(seed), 4)
    return {
        "point_data": draw_point_data(jax.random.fold_in(arg_keys[3], 71), 0),
        "right_side": draw_right_side(jax.random.fold_in(arg_keys[3], 71), 0),
        "pair_list": draw_pair_list(jax.random.fold_in(arg_keys[3], 71), 0),
    }


long_range = 1.0
short_range = 0.35
nugget = 1.0
pair_batch = 64
diagonal_batch = 16

def wendland(distance, reach):
    scaled = distance / reach
    remain = jnp.maximum(1.0 - scaled, 0.0)
    square = remain * remain
    return square * square * (4.0 * scaled + 1.0)

def covariance_tiles(row_points, column_points):
    delta_x = row_points[:, 0, :, None] - column_points[:, 0, None, :]
    delta_y = row_points[:, 1, :, None] - column_points[:, 1, None, :]
    delta_z = row_points[:, 2, :, None] - column_points[:, 2, None, :]
    distance = jnp.sqrt(delta_x * delta_x + delta_y * delta_y + delta_z * delta_z)
    kernel = wendland(distance, long_range) + wendland(distance, short_range)
    return row_points[:, 3, :, None] * kernel * column_points[:, 3, None, :]

def round_tiles(values):
    return lax.optimization_barrier(values.astype(jnp.bfloat16)).astype(jnp.float32)

def apply_operator(direction, blocks, lower_block, upper_block, keep_pair):
    rounded = round_tiles(direction)
    direction_blocks = rounded.reshape(COLS, NB, BLOCK)
    diagonal_points = blocks.reshape(NB // diagonal_batch, diagonal_batch, 4, BLOCK)
    diagonal_dirs = direction_blocks.reshape(COLS, NB // diagonal_batch, diagonal_batch, BLOCK).transpose(1, 0, 2, 3)

    def diagonal_step(inputs):
        points_here, dirs_here = inputs
        tiles_here = round_tiles(covariance_tiles(points_here, points_here))
        return jnp.einsum('tij,ctj->cti', tiles_here, dirs_here)
    diagonal = lax.map(diagonal_step, (diagonal_points, diagonal_dirs))
    diagonal = diagonal.transpose(1, 0, 2, 3).reshape(COLS, NB * BLOCK)

    def pair_step(totals, inputs):
        low_here, high_here, keep_here = inputs
        tiles_here = covariance_tiles(blocks[low_here], blocks[high_here])
        tiles_here = round_tiles(jnp.where(keep_here[:, None, None], tiles_here, 0.0))
        totals = totals.at[:, low_here].add(jnp.einsum('tij,ctj->cti', tiles_here, direction_blocks[:, high_here]))
        totals = totals.at[:, high_here].add(jnp.einsum('tij,cti->ctj', tiles_here, direction_blocks[:, low_here]))
        return (totals, None)
    empty = jnp.zeros((COLS, NB, BLOCK), jnp.float32)
    totals, _ = lax.scan(pair_step, empty, (lower_block, upper_block, keep_pair))
    return nugget * direction + diagonal + totals.reshape(COLS, NB * BLOCK)

def reference(point_data, right_side, pair_list):
    blocks = point_data.reshape(4, NB, BLOCK).transpose(1, 0, 2)
    listed = pair_list.shape[1]
    padded = (listed + pair_batch - 1) // pair_batch * pair_batch
    filler = jnp.zeros((padded - listed,), jnp.int32)
    lower_block = jnp.concatenate([pair_list[0].astype(jnp.int32), filler]).reshape(-1, pair_batch)
    upper_block = jnp.concatenate([pair_list[1].astype(jnp.int32), filler]).reshape(-1, pair_batch)
    keep_pair = (jnp.arange(padded) < listed).reshape(-1, pair_batch)
    solution = jnp.zeros_like(right_side)
    residual = right_side
    direction = right_side
    norm_now = lax.optimization_barrier(jnp.sum(residual * residual, axis=1))
    for step in range(ITERS):
        image = apply_operator(direction, blocks, lower_block, upper_block, keep_pair)
        alpha = norm_now / lax.optimization_barrier(jnp.sum(direction * image, axis=1))
        solution = solution + alpha[:, None] * direction
        residual = residual - alpha[:, None] * image
        if step + 1 < ITERS:
            norm_next = lax.optimization_barrier(jnp.sum(residual * residual, axis=1))
            direction = residual + (norm_next / norm_now)[:, None] * direction
            norm_now = norm_next
    return (solution, residual)
```

```python
import functools

import jax
import jax.numpy as jnp
from jax import lax
from jax.experimental import pallas as pl
from jax.experimental.pallas import tpu as pltpu
from jax.sharding import PartitionSpec as P

SIDE = 4
BLOCK = 128
MESH = pl.DeviceIdType.MESH
long_range = 1.0
short_range = 0.35
nugget = 1.0
PHASES = 26


def covariance(xj, yj, zj, sj, xi, yi, zi, si):
    dx, dy, dz = xj - xi, yj - yi, zj - zi
    d = jnp.sqrt(dx * dx + dy * dy + dz * dz)

    def wendland(u):
        remain = jnp.maximum(1.0 - u, 0.0)
        square = remain * remain
        return square * square * (4.0 * u + 1.0)

    return sj * (wendland(d * (1.0 / long_range)) + wendland(d * (1.0 / short_range))) * si


def kernel(side, depth, point_ref, right_ref, solution_ref, residual_ref,
           g_pts, g_vec0, g_vec1, g_vec2, g_vec3, line_pts, zs_pts, zr_pts, zs_vec, zr_vec, h_pts, h_vec,
           tiles, p_all, r_all, ar_one, ar_two, table_v, table_s, coef, send, recv, local_sem):
    g_vec = (g_vec0, g_vec1, g_vec2, g_vec3)
    chips = side * side
    slots = 4 * chips
    zslots = 2 * depth
    R = right_ref.shape[0]
    my_z = lax.axis_index("row")
    my_col = lax.axis_index("col")
    core = my_col % 2
    chip = my_col // 2
    xx = chip % side
    yy = chip // side
    zs = my_z * 2 + core
    own = (core * chips + chip) * 2

    def device(zslot, chip_):
        return (zslot // 2, chip_ * 2 + zslot % 2)

    def shifted(ox, oy):
        return ((yy + oy) % side) * side + (xx + ox) % side

    def plane_peer(o):
        return device(zs, shifted(o % side, o // side))

    def line_peer(o):
        return device((my_z + o) % depth * 2 + core, chip)

    def pillar_peer(o):
        return device((zs + o) % zslots, chip)

    def neighbour(n, oz):
        return device((zs + oz + zslots) % zslots, shifted(n // 3 - 1 + side, n % 3 - 1 + side))

    def push(src, dst, phase, peer):
        pltpu.make_async_remote_copy(
            src_ref=src, dst_ref=dst, send_sem=send.at[phase], recv_sem=recv.at[phase],
            device_id=peer, device_id_type=MESH,
        ).start()

    phases = []

    def new_phase(view):
        phases.append(view)
        return len(phases) - 1

    def arrived(phase):
        view = phases[phase]
        pltpu.make_async_copy(view, view, recv.at[phase]).wait()

    def loop(lo, hi, body):
        lax.fori_loop(lo, hi, lambda i, c: (body(i), c)[1], 0)

    def plane_start(buf):
        phase = new_phase(buf.at[pl.ds(0, 2 * (chips - 1))])
        part = buf.at[pl.ds(own, 2)]
        loop(1, chips, lambda o: push(part, part, phase, plane_peer(o)))
        return phase

    def forward_start(buf):
        phase = new_phase(buf.at[pl.ds(0, 2 * chips)])
        part = buf.at[pl.ds(core * 2 * chips, 2 * chips)]
        push(part, part, phase, device(my_z * 2 + 1 - core, chip))
        return phase

    def column_start(buf, staged, into, table):
        phase = new_phase(into.at[pl.ds(0, 2 * (depth - 1))])

        def select(t):
            staged[t] = buf[table_s[table, 4, t]]

        loop(0, 2 * depth, select)
        into[2 * my_z] = staged[2 * my_z]
        into[2 * my_z + 1] = staged[2 * my_z + 1]

        def one(o):
            z_to = (my_z + o) % depth
            push(staged.at[pl.ds(2 * z_to, 2)], into.at[pl.ds(2 * my_z, 2)], phase, line_peer(o))

        loop(1, depth, one)
        return phase

    def column_sum(into):
        pair = []
        for half in range(2):
            total = into[half].astype(jnp.float32)
            for z in range(1, depth):
                total = total + into[2 * z + half].astype(jnp.float32)
            pair.append(total)
        return pair

    def halo_start(buf):
        phase = new_phase(buf.at[pl.ds(0, 34)])

        def one(n):
            there = (8 - n) * 4

            @pl.when(n != 4)
            def _():
                push(buf.at[pl.ds(17, 2)], buf.at[pl.ds(there + 1, 2)], phase, neighbour(n, 0))

            push(buf.at[pl.ds(18, 1)], buf.at[pl.ds(there, 1)], phase, neighbour(n, 1))
            push(buf.at[pl.ds(17, 1)], buf.at[pl.ds(there + 3, 1)], phase, neighbour(n, -1))

        loop(0, 9, one)
        return phase

    pts = point_ref[...]
    for half in range(2):
        here = pts[:, half * BLOCK:(half + 1) * BLOCK]
        low = jnp.broadcast_to(jnp.floor(jnp.min(here, axis=1, keepdims=True)), (4, BLOCK))
        cx = jnp.clip(low[0:1], 0.0, side - 1.0)
        cy = jnp.clip(low[1:2], 0.0, side - 1.0)
        cz = jnp.clip(low[2:3], 0.0, 4.0 * depth - 1.0)
        slab = jnp.floor(cz * 0.25)
        level = cz - 4.0 * slab
        upper = jnp.floor(level * 0.5)
        slot = (upper * chips + cy * side + cx) * 2.0 + (level - 2.0 * upper)
        g_pts[own + half] = jnp.zeros((8, BLOCK), jnp.float32)
        g_pts[own + half, 0:4, :] = here
        g_pts[own + half, 4:5, :] = slab * slots + slot
        g_pts[own + half, 5:6, :] = slot
        g_pts[own + half, 6:7, :] = slab
        g_vec[0][own + half] = right_ref[:, half * BLOCK:(half + 1) * BLOCK].astype(jnp.bfloat16)
        line_pts[2 * my_z + half] = g_pts[own + half]
    g_pts[slots] = jnp.zeros((8, BLOCK), jnp.float32)
    for v in range(4):
        g_vec[v][slots] = jnp.zeros((R, BLOCK), jnp.bfloat16)

    barrier = pltpu.get_barrier_semaphore()

    def greet(peer):
        pl.semaphore_signal(barrier, inc=1, device_id=peer, device_id_type=MESH)

    loop(1, chips, lambda o: greet(plane_peer(o)))
    loop(1, zslots, lambda o: greet(pillar_peer(o)))

    def greet_three(n):
        @pl.when(n != 4)
        def _():
            greet(neighbour(n, 0))

        greet(neighbour(n, 1))
        greet(neighbour(n, -1))

    loop(0, 9, greet_three)
    pl.semaphore_wait(barrier, chips - 1 + zslots - 1 + 26)

    pts_plane = plane_start(g_pts)
    line = new_phase(line_pts.at[pl.ds(0, 2 * (depth - 1))])
    mine = line_pts.at[pl.ds(2 * my_z, 2)]
    loop(1, depth, lambda o: push(mine, mine, line, line_peer(o)))
    b_plane = plane_start(g_vec[0])
    arrived(pts_plane)
    pts_forward = forward_start(g_pts)
    arrived(line)
    arrived(pts_forward)

    lane = lax.broadcasted_iota(jnp.int32, (8, BLOCK), 1)
    target = ((lane // 2) * slots + (own + lane % 2)).astype(jnp.float32)
    gap = jnp.float32(slots)

    def find(k, acc):
        return jnp.minimum(acc, jnp.where(g_pts[k] == target, lax.convert_element_type(k, jnp.float32), gap))

    into_cells = lax.fori_loop(0, slots, find, jnp.full((8, BLOCK), gap, jnp.float32))
    table_v[0] = jnp.clip(into_cells.astype(jnp.int32), 0, slots)
    slab_here = lax.convert_element_type(my_z, jnp.float32)

    def place(t, acc):
        tile = line_pts[t]
        value = jnp.where(tile[6:7] == slab_here, tile[5:6], gap)
        return jnp.where(lane == t, jnp.broadcast_to(value, (8, BLOCK)), acc)

    into_homes = lax.fori_loop(0, 2 * depth, place, jnp.full((8, BLOCK), gap, jnp.float32))
    table_v[1] = jnp.clip(into_homes.astype(jnp.int32), 0, slots)
    copy = pltpu.make_async_copy(table_v, table_s, local_sem)
    copy.start()
    copy.wait()

    pts_column = column_start(g_pts, zs_pts, zr_pts, 0)
    arrived(b_plane)
    b_forward = forward_start(g_vec[0])
    arrived(pts_column)
    for half, total in enumerate(column_sum(zr_pts)):
        h_pts[17 + half] = total
    pts_halo = halo_start(h_pts)
    arrived(b_forward)
    b_column = column_start(g_vec[0], zs_vec.at[0], zr_vec.at[0], 0)
    arrived(pts_halo)

    def tile_column(n):
        for level in range(4):
            other = jnp.transpose(h_pts[n * 4 + level])
            xj, yj, zj, sj = (other[:, a:a + 1] for a in range(4))
            for half in range(2):
                rows, lanes = pl.ds(level * BLOCK, BLOCK), pl.ds(half * BLOCK, BLOCK)
                if not 0 <= level - half <= 2:
                    tiles[n, rows, lanes] = jnp.zeros((BLOCK, BLOCK), jnp.bfloat16)
                    continue
                xi, yi, zi, si = (h_pts[17 + half, a:a + 1, :] for a in range(4))
                tiles[n, rows, lanes] = covariance(xj, yj, zj, sj, xi, yi, zi, si).astype(jnp.bfloat16)

    loop(0, 9, tile_column)

    arrived(b_column)
    for half, total in enumerate(column_sum(zr_vec.at[0])):
        h_vec[0, 17 + half] = total.astype(jnp.bfloat16)
    halo = halo_start(h_vec.at[0])

    eye = lax.broadcasted_iota(jnp.int32, (R, BLOCK), 0) == lax.broadcasted_iota(jnp.int32, (R, BLOCK), 1)
    row8 = lax.broadcasted_iota(jnp.int32, (8, BLOCK), 0)

    def as_lanes(a, b):
        total = jnp.sum(a * b, axis=1, keepdims=True)
        return jnp.sum(jnp.where(eye, total, 0.0), axis=0, keepdims=True)

    def as_rows(values):
        column = jnp.sum(jnp.where(eye, values, 0.0), axis=1, keepdims=True)
        return jnp.broadcast_to(column, (R, BLOCK))

    def sum_start(step, rows):
        tile = jnp.zeros((8, BLOCK), jnp.float32)
        for i, value in enumerate(rows):
            tile = jnp.where(row8 == i, value, tile)
        buf = ar_one.at[step]
        buf[chip] = tile
        phase = new_phase(buf.at[pl.ds(0, chips - 1)])
        part = buf.at[pl.ds(chip, 1)]
        loop(1, chips, lambda o: push(part, part, phase, plane_peer(o)))
        return phase

    def sum_second(step, phase):
        arrived(phase)
        buf, second = ar_one.at[step], ar_two.at[step]
        total = buf[0]
        for i in range(1, chips):
            total = total + buf[i]
        second[zs] = total
        phase = new_phase(second.at[pl.ds(0, zslots - 1)])
        part = second.at[pl.ds(zs, 1)]
        loop(1, zslots, lambda o: push(part, part, phase, pillar_peer(o)))
        return phase

    def sum_finish(step, phase):
        arrived(phase)
        second = ar_two.at[step]
        total = second[0]
        for i in range(1, zslots):
            total = total + second[i]
        return total

    planes, forwards, columns = {}, {}, {}
    norm_now = None
    for step in range(3):
        arrived(halo)

        def column(n, acc, step=step):
            parts = []
            for level in range(4):
                k = n * 4 + level
                if step == 0:
                    parts.append(h_vec[0, k])
                    continue
                if step == 1:
                    p_old = h_vec[0, k].astype(jnp.float32)
                    r_old = p_old
                else:
                    p_old, r_old = p_all[k], r_all[k]
                image = nugget * p_old + h_vec[step, k].astype(jnp.float32)
                r_new = r_old - coef[2 * step - 2] * image
                p_new = r_new + coef[2 * step - 1] * p_old
                r_all[k] = r_new
                p_all[k] = p_new
                parts.append(p_new.astype(jnp.bfloat16))
            lhs = jnp.concatenate(parts, axis=1)
            return acc + jnp.dot(lhs, tiles[n], preferred_element_type=jnp.float32)

        product = lax.fori_loop(0, 9, column, jnp.zeros((R, 2 * BLOCK), jnp.float32))
        pq = rq = qq = rr = jnp.zeros((R, BLOCK), jnp.float32)
        for half in range(2):
            if step == 0:
                p_own = h_vec[0, 17 + half].astype(jnp.float32)
                r_own = p_own
            else:
                p_own, r_own = p_all[17 + half], r_all[17 + half]
            rounded = product[:, half * BLOCK:(half + 1) * BLOCK].astype(jnp.bfloat16)
            g_vec[step + 1][own + half] = rounded
            if step < 2:
                h_vec[step + 1, 17 + half] = rounded
            q = nugget * p_own + rounded.astype(jnp.float32)
            pq, rq, qq = pq + p_own * q, rq + r_own * q, qq + q * q
            rr = rr + r_own * r_own
        if step < 2:
            halo = halo_start(h_vec.at[step + 1])
        one = jnp.float32(1.0)
        rows = [as_lanes(a, one) for a in ((pq, rq, qq, rr) if step == 0 else (pq, rq, qq))]
        ar = sum_start(step, rows)
        planes[step] = plane_start(g_vec[step + 1])
        if step > 0:
            arrived(planes[step - 1])
            forwards[step - 1] = forward_start(g_vec[step])
        ar = sum_second(step, ar)
        if step > 0:
            arrived(forwards[step - 1])
            columns[step - 1] = column_start(g_vec[step], zs_vec.at[step], zr_vec.at[step], 1)
        totals = sum_finish(step, ar)
        if step == 0:
            norm_now = totals[3:4]
        alpha = norm_now / totals[0:1]
        norm_next = jnp.maximum(norm_now - 2.0 * alpha * totals[1:2] + alpha * alpha * totals[2:3], 0.0)
        coef[2 * step] = as_rows(alpha)
        coef[2 * step + 1] = as_rows(norm_next / norm_now)
        norm_now = norm_next

    arrived(planes[2])
    forwards[2] = forward_start(g_vec[3])
    arrived(forwards[2])
    columns[2] = column_start(g_vec[3], zs_vec.at[3], zr_vec.at[3], 1)
    for step in range(3):
        arrived(columns[step])
    images = [column_sum(zr_vec.at[step + 1]) for step in range(3)]
    for half in range(2):
        lanes = pl.ds(half * BLOCK, BLOCK)
        residual = direction = right_ref[:, lanes]
        total = jnp.zeros_like(residual)
        for step in range(3):
            total = total + coef[2 * step] * direction
            residual = residual - coef[2 * step] * (nugget * direction + images[step][half])
            if step < 2:
                direction = residual + coef[2 * step + 1] * direction
        solution_ref[:, lanes] = total
        residual_ref[:, lanes] = residual

    assert len(phases) == PHASES
    for phase, view in enumerate(phases):
        pltpu.make_async_copy(view, view, send.at[phase]).wait()


def per_device(side, depth, point_data, right_side, pair_list):
    R = right_side.shape[0]
    chips = side * side
    f32, bf16 = jnp.float32, jnp.bfloat16
    vmem = pl.BlockSpec(memory_space=pltpu.VMEM)
    out = jax.ShapeDtypeStruct(right_side.shape, f32)
    return pl.pallas_call(
        functools.partial(kernel, side, depth),
        out_shape=(out, out),
        in_specs=[vmem, vmem],
        out_specs=(vmem, vmem),
        scratch_shapes=[
            pltpu.VMEM((4 * chips + 1, 8, BLOCK), f32),
            *[pltpu.VMEM((4 * chips + 1, R, BLOCK), bf16)] * 4,
            pltpu.VMEM((2 * depth, 8, BLOCK), f32),
            pltpu.VMEM((2 * depth, 8, BLOCK), f32),
            pltpu.VMEM((2 * depth, 8, BLOCK), f32),
            pltpu.VMEM((4, 2 * depth, R, BLOCK), bf16),
            pltpu.VMEM((4, 2 * depth, R, BLOCK), bf16),
            pltpu.VMEM((36, 8, BLOCK), f32),
            pltpu.VMEM((3, 36, R, BLOCK), bf16),
            pltpu.VMEM((9, 4 * BLOCK, 2 * BLOCK), bf16),
            pltpu.VMEM((36, R, BLOCK), f32),
            pltpu.VMEM((36, R, BLOCK), f32),
            pltpu.VMEM((3, chips, 8, BLOCK), f32),
            pltpu.VMEM((3, 2 * depth, 8, BLOCK), f32),
            pltpu.VMEM((2, 8, BLOCK), jnp.int32),
            pltpu.SMEM((2, 8, BLOCK), jnp.int32),
            pltpu.VMEM((6, R, BLOCK), f32),
            pltpu.SemaphoreType.DMA((PHASES,)),
            pltpu.SemaphoreType.DMA((PHASES,)),
            pltpu.SemaphoreType.DMA,
        ],
        compiler_params=pltpu.CompilerParams(
            collective_id=0, has_side_effects=True, vmem_limit_bytes=40 << 20
        ),
    )(point_data, right_side)


def build(mesh, side):
    depth = mesh.shape["row"]
    placed = P(None, ("row", "col"))
    return jax.shard_map(
        functools.partial(per_device, side, depth),
        mesh=mesh,
        in_specs=(placed, placed, P()),
        out_specs=(placed, placed),
        check_vma=False,
    )


def solution(mesh):
    return build(mesh, SIDE)
```

```python
import functools

import jax
import jax.numpy as jnp
from jax import lax
from jax.experimental import pallas as pl
from jax.experimental.pallas import tpu as pltpu
from jax.sharding import PartitionSpec as P

SIDE = 4
BLOCK = 128
MESH = pl.DeviceIdType.MESH
long_range = 1.0
short_range = 0.35
nugget = 1.0
CHUNKS = (4, 1, 1, 4)
PHASES = 14 + 3 * sum(CHUNKS)


def covariance(xj, yj, zj, sj, xi, yi, zi, si):
    dx, dy, dz = xj - xi, yj - yi, zj - zi
    d = jnp.sqrt(dx * dx + dy * dy + dz * dz)

    def wendland(u):
        remain = jnp.maximum(1.0 - u, 0.0)
        square = remain * remain
        return square * square * (4.0 * u + 1.0)

    return sj * (wendland(d * (1.0 / long_range)) + wendland(d * (1.0 / short_range))) * si


def kernel(side, depth, point_ref, right_ref, solution_ref, residual_ref, *scratch):
    chips = side * side
    slots = 4 * chips
    zslots = 2 * depth
    R = right_ref.shape[0]
    g_vec = [list(scratch[sum(CHUNKS[:v]):sum(CHUNKS[:v + 1])]) for v in range(4)]
    zs_vec = scratch[sum(CHUNKS):sum(CHUNKS) + 4]
    zr_vec = scratch[sum(CHUNKS) + 4:sum(CHUNKS) + 8]
    (g_pts, line_pts, zs_pts, zr_pts, h_pts, h_vec, tiles, p_all, r_all, ar_one, ar_two,
     table_v, table_s, coef, send, recv, local_sem) = scratch[sum(CHUNKS) + 8:]
    my_z = lax.axis_index("row")
    my_col = lax.axis_index("col")
    core = my_col % 2
    chip = my_col // 2
    xx = chip % side
    yy = chip // side
    zs = my_z * 2 + core
    own = (core * chips + chip) * 2
    sibling = (my_z, chip * 2 + 1 - core)

    def rows_of(v, ch):
        size = R // CHUNKS[v]
        return pl.ds(ch * size, size)

    def device(zslot, chip_):
        return (zslot // 2, chip_ * 2 + zslot % 2)

    def shifted(ox, oy):
        return ((yy + oy) % side) * side + (xx + ox) % side

    def plane_peer(o):
        return device(zs, shifted(o % side, o // side))

    def line_peer(o):
        return device((my_z + o) % depth * 2 + core, chip)

    def pillar_peer(o):
        return device((zs + o) % zslots, chip)

    def neighbour(n, oz):
        return device((zs + oz + zslots) % zslots, shifted(n // 3 - 1 + side, n % 3 - 1 + side))

    def push(src, dst, phase, peer):
        pltpu.make_async_remote_copy(
            src_ref=src, dst_ref=dst, send_sem=send.at[phase], recv_sem=recv.at[phase],
            device_id=peer, device_id_type=MESH,
        ).start()

    phases = []

    def new_phase(view):
        phases.append(view)
        return len(phases) - 1

    def arrived(phase):
        view = phases[phase]
        pltpu.make_async_copy(view, view, recv.at[phase]).wait()

    def loop(lo, hi, body):
        lax.fori_loop(lo, hi, lambda i, c: (body(i), c)[1], 0)

    def plane_start(buf):
        phase = new_phase(buf.at[pl.ds(0, 2 * (chips - 1))])
        part = buf.at[pl.ds(own, 2)]
        loop(1, chips, lambda o: push(part, part, phase, plane_peer(o)))
        return phase

    def forward_start(buf):
        phase = new_phase(buf.at[pl.ds(0, 2 * chips)])
        part = buf.at[pl.ds(core * 2 * chips, 2 * chips)]
        push(part, part, phase, sibling)
        return phase

    def column_start(buf, staged, into, table):
        phase = new_phase(into.at[pl.ds(0, 2 * (depth - 1))])
        for t in range(2 * depth):
            staged[t] = buf[table_s[table, 4, t]]
        into[2 * my_z] = staged[2 * my_z]
        into[2 * my_z + 1] = staged[2 * my_z + 1]

        def one(o):
            z_to = (my_z + o) % depth
            push(staged.at[pl.ds(2 * z_to, 2)], into.at[pl.ds(2 * my_z, 2)], phase, line_peer(o))

        loop(1, depth, one)
        return phase

    def column_sum(into):
        pair = []
        for half in range(2):
            total = into[half].astype(jnp.float32)
            for z in range(1, depth):
                total = total + into[2 * z + half].astype(jnp.float32)
            pair.append(total)
        return pair

    def halo_start(buf):
        phase = new_phase(buf.at[pl.ds(0, 34)])

        def one(n):
            there = (8 - n) * 4

            @pl.when(n != 4)
            def _():
                push(buf.at[pl.ds(17, 2)], buf.at[pl.ds(there + 1, 2)], phase, neighbour(n, 0))

            push(buf.at[pl.ds(18, 1)], buf.at[pl.ds(there, 1)], phase, neighbour(n, 1))
            push(buf.at[pl.ds(17, 1)], buf.at[pl.ds(there + 3, 1)], phase, neighbour(n, -1))

        loop(0, 9, one)
        return phase

    class Journey:
        def __init__(self, v, table):
            self.v, self.table, self.count = v, table, CHUNKS[v]
            self.planes = [plane_start(buf) for buf in g_vec[v]]
            self.forwards, self.columns = [], []

        def forward(self):
            ch = len(self.forwards)
            arrived(self.planes[ch])
            self.forwards.append(forward_start(g_vec[self.v][ch]))

        def column(self):
            ch = len(self.columns)
            arrived(self.forwards[ch])
            self.columns.append(column_start(
                g_vec[self.v][ch], zs_vec[self.v].at[ch], zr_vec[self.v].at[ch], self.table))

        def through(self):
            self.forward()
            for _ in range(1, self.count):
                self.forward()
                self.column()
            self.column()

        def sums(self, ch):
            arrived(self.columns[ch])
            return column_sum(zr_vec[self.v].at[ch])

    pts = point_ref[...]
    for half in range(2):
        here = pts[:, half * BLOCK:(half + 1) * BLOCK]
        low = jnp.broadcast_to(jnp.floor(jnp.min(here, axis=1, keepdims=True)), (4, BLOCK))
        cx = jnp.clip(low[0:1], 0.0, side - 1.0)
        cy = jnp.clip(low[1:2], 0.0, side - 1.0)
        cz = jnp.clip(low[2:3], 0.0, 4.0 * depth - 1.0)
        slab = jnp.floor(cz * 0.25)
        level = cz - 4.0 * slab
        upper = jnp.floor(level * 0.5)
        slot = (upper * chips + cy * side + cx) * 2.0 + (level - 2.0 * upper)
        g_pts[own + half] = jnp.zeros((8, BLOCK), jnp.float32)
        g_pts[own + half, 0:4, :] = here
        g_pts[own + half, 4:5, :] = slab * slots + slot
        g_pts[own + half, 5:6, :] = slot
        g_pts[own + half, 6:7, :] = slab
        line_pts[2 * my_z + half] = g_pts[own + half]
        for ch in range(CHUNKS[0]):
            part = right_ref[rows_of(0, ch), half * BLOCK:(half + 1) * BLOCK]
            g_vec[0][ch][own + half] = part.astype(jnp.bfloat16)
    g_pts[slots] = jnp.zeros((8, BLOCK), jnp.float32)
    for v in range(4):
        for buf in g_vec[v]:
            buf[slots] = jnp.zeros((R // CHUNKS[v], BLOCK), jnp.bfloat16)

    barrier = pltpu.get_barrier_semaphore()

    def greet(peer):
        pl.semaphore_signal(barrier, inc=1, device_id=peer, device_id_type=MESH)

    loop(1, chips, lambda o: greet(plane_peer(o)))
    loop(1, depth, lambda o: greet(line_peer(o)))
    greet(sibling)
    pl.semaphore_wait(barrier, chips - 1 + depth - 1 + 1)

    pts_plane = plane_start(g_pts)
    line = new_phase(line_pts.at[pl.ds(0, 2 * (depth - 1))])
    mine = line_pts.at[pl.ds(2 * my_z, 2)]
    loop(1, depth, lambda o: push(mine, mine, line, line_peer(o)))
    inward = Journey(0, 0)
    arrived(pts_plane)
    pts_forward = forward_start(g_pts)
    arrived(line)

    lane = lax.broadcasted_iota(jnp.int32, (8, BLOCK), 1)
    target = ((lane // 2) * slots + (own + lane % 2)).astype(jnp.float32)
    gap = jnp.float32(slots)
    slab_here = lax.convert_element_type(my_z, jnp.float32)
    acc = jnp.full((8, BLOCK), gap, jnp.float32)
    for t in range(2 * depth):
        tile = line_pts[t]
        value = jnp.where(tile[6:7] == slab_here, tile[5:6], gap)
        acc = jnp.where(lane == t, jnp.broadcast_to(value, (8, BLOCK)), acc)
    table_v[1] = jnp.clip(acc.astype(jnp.int32), 0, slots)

    arrived(pts_forward)
    acc = jnp.full((8, BLOCK), gap, jnp.float32)
    for k in range(slots):
        acc = jnp.minimum(acc, jnp.where(g_pts[k] == target, jnp.float32(k), gap))
    table_v[0] = jnp.clip(acc.astype(jnp.int32), 0, slots)
    copy = pltpu.make_async_copy(table_v, table_s, local_sem)
    copy.start()
    copy.wait()

    pts_column = column_start(g_pts, zs_pts, zr_pts, 0)
    inward.through()
    arrived(pts_column)
    for half, total in enumerate(column_sum(zr_pts)):
        h_pts[17 + half] = total
    pts_halo = halo_start(h_pts)
    for ch in range(CHUNKS[0]):
        for half, total in enumerate(inward.sums(ch)):
            h_vec[0, 17 + half, rows_of(0, ch), :] = total.astype(jnp.bfloat16)
    halo = halo_start(h_vec.at[0])

    arrived(pts_halo)

    def tile_column(n):
        for level in range(4):
            other = jnp.transpose(h_pts[n * 4 + level])
            xj, yj, zj, sj = (other[:, a:a + 1] for a in range(4))
            for half in range(2):
                rows, lanes = pl.ds(level * BLOCK, BLOCK), pl.ds(half * BLOCK, BLOCK)
                if not 0 <= level - half <= 2:
                    tiles[n, rows, lanes] = jnp.zeros((BLOCK, BLOCK), jnp.bfloat16)
                    continue
                xi, yi, zi, si = (h_pts[17 + half, a:a + 1, :] for a in range(4))
                tiles[n, rows, lanes] = covariance(xj, yj, zj, sj, xi, yi, zi, si).astype(jnp.bfloat16)

    loop(0, 9, tile_column)

    eye = lax.broadcasted_iota(jnp.int32, (R, BLOCK), 0) == lax.broadcasted_iota(jnp.int32, (R, BLOCK), 1)
    row8 = lax.broadcasted_iota(jnp.int32, (8, BLOCK), 0)

    def as_lanes(values):
        total = jnp.sum(values, axis=1, keepdims=True)
        return jnp.sum(jnp.where(eye, total, 0.0), axis=0, keepdims=True)

    def as_rows(values):
        column = jnp.sum(jnp.where(eye, values, 0.0), axis=1, keepdims=True)
        return jnp.broadcast_to(column, (R, BLOCK))

    def sum_start(step, rows):
        tile = jnp.zeros((8, BLOCK), jnp.float32)
        for i, value in enumerate(rows):
            tile = jnp.where(row8 == i, value, tile)
        buf = ar_one.at[step]
        buf[chip] = tile
        phase = new_phase(buf.at[pl.ds(0, chips - 1)])
        part = buf.at[pl.ds(chip, 1)]
        loop(1, chips, lambda o: push(part, part, phase, plane_peer(o)))
        return phase

    def sum_second(step, phase):
        arrived(phase)
        buf, second = ar_one.at[step], ar_two.at[step]
        total = buf[0]
        for i in range(1, chips):
            total = total + buf[i]
        second[zs] = total
        phase = new_phase(second.at[pl.ds(0, zslots - 1)])
        part = second.at[pl.ds(zs, 1)]
        loop(1, zslots, lambda o: push(part, part, phase, pillar_peer(o)))
        return phase

    def sum_finish(step, phase):
        arrived(phase)
        second = ar_two.at[step]
        total = second[0]
        for i in range(1, zslots):
            total = total + second[i]
        return total

    outward = []
    norm_now = None
    for step in range(3):
        arrived(halo)
        product = jnp.zeros((R, 2 * BLOCK), jnp.float32)
        for n in range(9):
            parts = []
            for level in range(4):
                k = n * 4 + level
                if step == 0:
                    parts.append(h_vec[0, k])
                    continue
                if step == 1:
                    p_old = h_vec[0, k].astype(jnp.float32)
                    r_old = p_old
                else:
                    p_old, r_old = p_all[k], r_all[k]
                image = nugget * p_old + h_vec[step, k].astype(jnp.float32)
                r_new = r_old - coef[2 * step - 2] * image
                p_new = r_new + coef[2 * step - 1] * p_old
                r_all[k] = r_new
                p_all[k] = p_new
                parts.append(p_new.astype(jnp.bfloat16))
            lhs = jnp.concatenate(parts, axis=1)
            product = product + jnp.dot(lhs, tiles[n], preferred_element_type=jnp.float32)
        pq = rq = qq = rr = jnp.zeros((R, BLOCK), jnp.float32)
        for half in range(2):
            if step == 0:
                p_own = h_vec[0, 17 + half].astype(jnp.float32)
                r_own = p_own
            else:
                p_own, r_own = p_all[17 + half], r_all[17 + half]
            rounded = product[:, half * BLOCK:(half + 1) * BLOCK].astype(jnp.bfloat16)
            if step < 2:
                h_vec[step + 1, 17 + half] = rounded
            for ch in range(CHUNKS[step + 1]):
                size = R // CHUNKS[step + 1]
                g_vec[step + 1][ch][own + half] = rounded[ch * size:(ch + 1) * size]
            q = nugget * p_own + rounded.astype(jnp.float32)
            pq, rq, qq = pq + p_own * q, rq + r_own * q, qq + q * q
            rr = rr + r_own * r_own
        rows = [as_lanes(a) for a in ((pq, rq, qq, rr) if step == 0 else (pq, rq, qq))]
        ar = sum_start(step, rows)
        if step < 2:
            halo = halo_start(h_vec.at[step + 1])
        outward.append(Journey(step + 1, 1))
        if step == 1:
            outward[0].forward()
        ar = sum_second(step, ar)
        if step == 1:
            outward[0].column()
        if step == 2:
            outward[1].forward()
            outward[2].through()
            outward[1].column()
        totals = sum_finish(step, ar)
        if step == 0:
            norm_now = totals[3:4]
        alpha = norm_now / totals[0:1]
        coef[2 * step] = as_rows(alpha)
        if step < 2:
            norm_next = norm_now - 2.0 * alpha * totals[1:2] + alpha * alpha * totals[2:3]
            norm_next = jnp.maximum(norm_next, 0.0)
            coef[2 * step + 1] = as_rows(norm_next / norm_now)
            norm_now = norm_next

    images = [outward[step].sums(0) for step in range(2)]
    for ch in range(CHUNKS[3]):
        last = outward[2].sums(ch)
        rows = rows_of(3, ch)
        size = R // CHUNKS[3]
        cut = slice(ch * size, (ch + 1) * size)
        for half in range(2):
            lanes = pl.ds(half * BLOCK, BLOCK)
            residual = direction = right_ref[rows, lanes]
            total = jnp.zeros_like(residual)
            for step in range(3):
                image = last[half] if step == 2 else images[step][half][cut]
                total = total + coef[2 * step, rows, :] * direction
                residual = residual - coef[2 * step, rows, :] * (nugget * direction + image)
                if step < 2:
                    direction = residual + coef[2 * step + 1, rows, :] * direction
            solution_ref[rows, lanes] = total
            residual_ref[rows, lanes] = residual

    assert len(phases) == PHASES
    for phase, view in enumerate(phases):
        pltpu.make_async_copy(view, view, send.at[phase]).wait()


def per_device(side, depth, point_data, right_side, pair_list):
    R = right_side.shape[0]
    chips = side * side
    f32, bf16 = jnp.float32, jnp.bfloat16
    vmem = pl.BlockSpec(memory_space=pltpu.VMEM)
    out = jax.ShapeDtypeStruct(right_side.shape, f32)
    return pl.pallas_call(
        functools.partial(kernel, side, depth),
        out_shape=(out, out),
        in_specs=[vmem, vmem],
        out_specs=(vmem, vmem),
        scratch_shapes=[
            *[pltpu.VMEM((4 * chips + 1, R // n, BLOCK), bf16) for n in CHUNKS for _ in range(n)],
            *[pltpu.VMEM((n, 2 * depth, R // n, BLOCK), bf16) for n in CHUNKS],
            *[pltpu.VMEM((n, 2 * depth, R // n, BLOCK), bf16) for n in CHUNKS],
            pltpu.VMEM((4 * chips + 1, 8, BLOCK), f32),
            pltpu.VMEM((2 * depth, 8, BLOCK), f32),
            pltpu.VMEM((2 * depth, 8, BLOCK), f32),
            pltpu.VMEM((2 * depth, 8, BLOCK), f32),
            pltpu.VMEM((36, 8, BLOCK), f32),
            pltpu.VMEM((3, 36, R, BLOCK), bf16),
            pltpu.VMEM((9, 4 * BLOCK, 2 * BLOCK), bf16),
            pltpu.VMEM((36, R, BLOCK), f32),
            pltpu.VMEM((36, R, BLOCK), f32),
            pltpu.VMEM((3, chips, 8, BLOCK), f32),
            pltpu.VMEM((3, 2 * depth, 8, BLOCK), f32),
            pltpu.VMEM((2, 8, BLOCK), jnp.int32),
            pltpu.SMEM((2, 8, BLOCK), jnp.int32),
            pltpu.VMEM((6, R, BLOCK), f32),
            pltpu.SemaphoreType.DMA((PHASES,)),
            pltpu.SemaphoreType.DMA((PHASES,)),
            pltpu.SemaphoreType.DMA,
        ],
        compiler_params=pltpu.CompilerParams(
            collective_id=0, has_side_effects=True, vmem_limit_bytes=40 << 20
        ),
    )(point_data, right_side)


def build(mesh, side):
    depth = mesh.shape["row"]
    placed = P(None, ("row", "col"))
    return jax.shard_map(
        functools.partial(per_device, side, depth),
        mesh=mesh,
        in_specs=(placed, placed, P()),
        out_specs=(placed, placed),
        check_vma=False,
    )


def solution(mesh):
    return build(mesh, SIDE)
```

```python
import functools

import jax
import jax.numpy as jnp
from jax import lax
from jax.experimental import pallas as pl
from jax.experimental.pallas import tpu as pltpu
from jax.sharding import PartitionSpec as P

SIDE = 4
BLOCK = 128
MESH = pl.DeviceIdType.MESH
long_range = 1.0
short_range = 0.35
nugget = 1.0
CHUNKS = (4, 1, 1, 4)
PHASES = 14 + 3 * sum(CHUNKS)


def covariance(xj, yj, zj, sj, xi, yi, zi, si):
    dx, dy, dz = xj - xi, yj - yi, zj - zi
    d = jnp.sqrt(dx * dx + dy * dy + dz * dz)

    def wendland(u):
        remain = jnp.maximum(1.0 - u, 0.0)
        square = remain * remain
        return square * square * (4.0 * u + 1.0)

    return sj * (wendland(d * (1.0 / long_range)) + wendland(d * (1.0 / short_range))) * si


def kernel(side, depth, point_hbm, right_hbm, solution_ref, residual_ref, *scratch):
    chips = side * side
    slots = 4 * chips
    zslots = 2 * depth
    R = right_hbm.shape[0]
    g_vec = [list(scratch[sum(CHUNKS[:v]):sum(CHUNKS[:v + 1])]) for v in range(4)]
    zs_vec = scratch[sum(CHUNKS):sum(CHUNKS) + 4]
    zr_vec = scratch[sum(CHUNKS) + 4:sum(CHUNKS) + 8]
    (g_pts, line_pts, zs_pts, zr_pts, h_pts, h_vec, tiles, p_all, r_all, ar_one, ar_two,
     table_v, table_s, coef, point_ref, right_ref, send, recv, local_sem) = scratch[sum(CHUNKS) + 8:]
    my_z = lax.axis_index("row")
    my_col = lax.axis_index("col")
    core = my_col % 2
    chip = my_col // 2
    xx = chip % side
    yy = chip // side
    zs = my_z * 2 + core
    own = (core * chips + chip) * 2
    sibling = (my_z, chip * 2 + 1 - core)

    def rows_of(v, ch):
        size = R // CHUNKS[v]
        return pl.ds(ch * size, size)

    def device(zslot, chip_):
        return (zslot // 2, chip_ * 2 + zslot % 2)

    def shifted(ox, oy):
        return ((yy + oy) % side) * side + (xx + ox) % side

    def plane_peer(o):
        return device(zs, shifted(o % side, o // side))

    def line_peer(o):
        return device((my_z + o) % depth * 2 + core, chip)

    def pillar_peer(o):
        return device((zs + o) % zslots, chip)

    def neighbour(n, oz):
        return device((zs + oz + zslots) % zslots, shifted(n // 3 - 1 + side, n % 3 - 1 + side))

    def push(src, dst, phase, peer):
        pltpu.make_async_remote_copy(
            src_ref=src, dst_ref=dst, send_sem=send.at[phase], recv_sem=recv.at[phase],
            device_id=peer, device_id_type=MESH,
        ).start()

    phases = []

    def new_phase(view):
        phases.append(view)
        return len(phases) - 1

    def arrived(phase):
        view = phases[phase]
        pltpu.make_async_copy(view, view, recv.at[phase]).wait()

    def loop(lo, hi, body):
        lax.fori_loop(lo, hi, lambda i, c: (body(i), c)[1], 0)

    def plane_start(buf):
        phase = new_phase(buf.at[pl.ds(0, 2 * (chips - 1))])
        part = buf.at[pl.ds(own, 2)]
        loop(1, chips, lambda o: push(part, part, phase, plane_peer(o)))
        return phase

    def forward_start(buf):
        phase = new_phase(buf.at[pl.ds(0, 2 * chips)])
        part = buf.at[pl.ds(core * 2 * chips, 2 * chips)]
        push(part, part, phase, sibling)
        return phase

    def column_start(buf, staged, into, table):
        phase = new_phase(into.at[pl.ds(0, 2 * (depth - 1))])
        for t in range(2 * depth):
            staged[t] = buf[table_s[table, 4, t]]
        into[2 * my_z] = staged[2 * my_z]
        into[2 * my_z + 1] = staged[2 * my_z + 1]

        def one(o):
            z_to = (my_z + o) % depth
            push(staged.at[pl.ds(2 * z_to, 2)], into.at[pl.ds(2 * my_z, 2)], phase, line_peer(o))

        loop(1, depth, one)
        return phase

    def column_sum(into):
        pair = []
        for half in range(2):
            total = into[half].astype(jnp.float32)
            for z in range(1, depth):
                total = total + into[2 * z + half].astype(jnp.float32)
            pair.append(total)
        return pair

    def halo_start(buf):
        phase = new_phase(buf.at[pl.ds(0, 34)])

        def one(n):
            there = (8 - n) * 4

            @pl.when(n != 4)
            def _():
                push(buf.at[pl.ds(17, 2)], buf.at[pl.ds(there + 1, 2)], phase, neighbour(n, 0))

            push(buf.at[pl.ds(18, 1)], buf.at[pl.ds(there, 1)], phase, neighbour(n, 1))
            push(buf.at[pl.ds(17, 1)], buf.at[pl.ds(there + 3, 1)], phase, neighbour(n, -1))

        loop(0, 9, one)
        return phase

    class Journey:
        def __init__(self, v, table):
            self.v, self.table, self.count = v, table, CHUNKS[v]
            self.planes = [plane_start(buf) for buf in g_vec[v]]
            self.forwards, self.columns = [], []

        def forward(self):
            ch = len(self.forwards)
            arrived(self.planes[ch])
            self.forwards.append(forward_start(g_vec[self.v][ch]))

        def column(self):
            ch = len(self.columns)
            arrived(self.forwards[ch])
            self.columns.append(column_start(
                g_vec[self.v][ch], zs_vec[self.v].at[ch], zr_vec[self.v].at[ch], self.table))

        def through(self):
            self.forward()
            for _ in range(1, self.count):
                self.forward()
                self.column()
            self.column()

        def sums(self, ch):
            arrived(self.columns[ch])
            return column_sum(zr_vec[self.v].at[ch])

    load = [
        pltpu.make_async_copy(point_hbm, point_ref, local_sem.at[0]),
        pltpu.make_async_copy(right_hbm, right_ref, local_sem.at[1]),
    ]
    for copy in load:
        copy.start()

    barrier = pltpu.get_barrier_semaphore()

    def greet(peer):
        pl.semaphore_signal(barrier, inc=1, device_id=peer, device_id_type=MESH)

    loop(1, chips, lambda o: greet(plane_peer(o)))
    loop(1, depth, lambda o: greet(line_peer(o)))
    greet(sibling)
    load[0].wait()
    pts = point_ref[...]
    for half in range(2):
        here = pts[:, half * BLOCK:(half + 1) * BLOCK]
        low = jnp.broadcast_to(jnp.floor(jnp.min(here, axis=1, keepdims=True)), (4, BLOCK))
        cx = jnp.clip(low[0:1], 0.0, side - 1.0)
        cy = jnp.clip(low[1:2], 0.0, side - 1.0)
        cz = jnp.clip(low[2:3], 0.0, 4.0 * depth - 1.0)
        slab = jnp.floor(cz * 0.25)
        level = cz - 4.0 * slab
        upper = jnp.floor(level * 0.5)
        slot = (upper * chips + cy * side + cx) * 2.0 + (level - 2.0 * upper)
        g_pts[own + half] = jnp.zeros((8, BLOCK), jnp.float32)
        g_pts[own + half, 0:4, :] = here
        g_pts[own + half, 4:5, :] = slab * slots + slot
        g_pts[own + half, 5:6, :] = slot
        g_pts[own + half, 6:7, :] = slab
        line_pts[2 * my_z + half] = g_pts[own + half]
    load[1].wait()
    for half in range(2):
        for ch in range(CHUNKS[0]):
            part = right_ref[rows_of(0, ch), half * BLOCK:(half + 1) * BLOCK]
            g_vec[0][ch][own + half] = part.astype(jnp.bfloat16)
    g_pts[slots] = jnp.zeros((8, BLOCK), jnp.float32)
    for v in range(4):
        for buf in g_vec[v]:
            buf[slots] = jnp.zeros((R // CHUNKS[v], BLOCK), jnp.bfloat16)

    pl.semaphore_wait(barrier, chips - 1 + depth - 1 + 1)

    pts_plane = plane_start(g_pts)
    line = new_phase(line_pts.at[pl.ds(0, 2 * (depth - 1))])
    mine = line_pts.at[pl.ds(2 * my_z, 2)]
    loop(1, depth, lambda o: push(mine, mine, line, line_peer(o)))
    inward = Journey(0, 0)
    arrived(pts_plane)
    pts_forward = forward_start(g_pts)
    arrived(line)

    lane = lax.broadcasted_iota(jnp.int32, (8, BLOCK), 1)
    target = ((lane // 2) * slots + (own + lane % 2)).astype(jnp.float32)
    gap = jnp.float32(slots)
    slab_here = lax.convert_element_type(my_z, jnp.float32)
    acc = jnp.full((8, BLOCK), gap, jnp.float32)
    for t in range(2 * depth):
        tile = line_pts[t]
        value = jnp.where(tile[6:7] == slab_here, tile[5:6], gap)
        acc = jnp.where(lane == t, jnp.broadcast_to(value, (8, BLOCK)), acc)
    table_v[1] = jnp.clip(acc.astype(jnp.int32), 0, slots)

    arrived(pts_forward)
    acc = jnp.full((8, BLOCK), gap, jnp.float32)
    for k in range(slots):
        acc = jnp.minimum(acc, jnp.where(g_pts[k] == target, jnp.float32(k), gap))
    table_v[0] = jnp.clip(acc.astype(jnp.int32), 0, slots)
    copy = pltpu.make_async_copy(table_v, table_s, local_sem.at[0])
    copy.start()
    copy.wait()

    pts_column = column_start(g_pts, zs_pts, zr_pts, 0)
    inward.through()
    arrived(pts_column)
    for half, total in enumerate(column_sum(zr_pts)):
        h_pts[17 + half] = total
    pts_halo = halo_start(h_pts)
    for ch in range(CHUNKS[0]):
        for half, total in enumerate(inward.sums(ch)):
            h_vec[0, 17 + half, rows_of(0, ch), :] = total.astype(jnp.bfloat16)
    halo = halo_start(h_vec.at[0])

    arrived(pts_halo)

    def tile_column(n):
        for level in range(4):
            other = jnp.transpose(h_pts[n * 4 + level])
            xj, yj, zj, sj = (other[:, a:a + 1] for a in range(4))
            for half in range(2):
                rows, lanes = pl.ds(level * BLOCK, BLOCK), pl.ds(half * BLOCK, BLOCK)
                if not 0 <= level - half <= 2:
                    tiles[n, rows, lanes] = jnp.zeros((BLOCK, BLOCK), jnp.bfloat16)
                    continue
                xi, yi, zi, si = (h_pts[17 + half, a:a + 1, :] for a in range(4))
                tiles[n, rows, lanes] = covariance(xj, yj, zj, sj, xi, yi, zi, si).astype(jnp.bfloat16)

    loop(0, 9, tile_column)

    eye = lax.broadcasted_iota(jnp.int32, (R, BLOCK), 0) == lax.broadcasted_iota(jnp.int32, (R, BLOCK), 1)
    row4 = lax.broadcasted_iota(jnp.int32, (4, BLOCK), 0)

    def as_lanes(values):
        total = jnp.sum(values, axis=1, keepdims=True)
        return jnp.sum(jnp.where(eye, total, 0.0), axis=0, keepdims=True)

    def as_rows(values):
        column = jnp.sum(jnp.where(eye, values, 0.0), axis=1, keepdims=True)
        return jnp.broadcast_to(column, (R, BLOCK))

    def sum_start(step, rows):
        tile = jnp.zeros((4, BLOCK), jnp.float32)
        for i, value in enumerate(rows):
            tile = jnp.where(row4 == i, value, tile)
        buf = ar_one.at[step]
        buf[chip] = tile
        phase = new_phase(buf.at[pl.ds(0, chips - 1)])
        part = buf.at[pl.ds(chip, 1)]
        loop(1, chips, lambda o: push(part, part, phase, plane_peer(o)))
        return phase

    def sum_second(step, phase):
        arrived(phase)
        buf, second = ar_one.at[step], ar_two.at[step]
        total = buf[0]
        for i in range(1, chips):
            total = total + buf[i]
        second[zs] = total
        phase = new_phase(second.at[pl.ds(0, zslots - 1)])
        part = second.at[pl.ds(zs, 1)]
        loop(1, zslots, lambda o: push(part, part, phase, pillar_peer(o)))
        return phase

    def sum_finish(step, phase):
        arrived(phase)
        second = ar_two.at[step]
        total = second[0]
        for i in range(1, zslots):
            total = total + second[i]
        return total

    outward = []
    norm_now = None
    for step in range(3):
        arrived(halo)
        product = jnp.zeros((R, 2 * BLOCK), jnp.float32)
        for n in range(9):
            parts = []
            for level in range(4):
                k = n * 4 + level
                if step == 0:
                    parts.append(h_vec[0, k])
                    continue
                if step == 1:
                    p_old = h_vec[0, k].astype(jnp.float32)
                    r_old = p_old
                else:
                    p_old, r_old = p_all[k], r_all[k]
                image = nugget * p_old + h_vec[step, k].astype(jnp.float32)
                r_new = r_old - coef[2 * step - 2] * image
                p_new = r_new + coef[2 * step - 1] * p_old
                r_all[k] = r_new
                p_all[k] = p_new
                parts.append(p_new.astype(jnp.bfloat16))
            lhs = jnp.concatenate(parts, axis=1)
            product = product + jnp.dot(lhs, tiles[n], preferred_element_type=jnp.float32)
        pq = rq = qq = rr = jnp.zeros((R, BLOCK), jnp.float32)
        for half in range(2):
            if step == 0:
                p_own = h_vec[0, 17 + half].astype(jnp.float32)
                r_own = p_own
            else:
                p_own, r_own = p_all[17 + half], r_all[17 + half]
            rounded = product[:, half * BLOCK:(half + 1) * BLOCK].astype(jnp.bfloat16)
            if step < 2:
                h_vec[step + 1, 17 + half] = rounded
            for ch in range(CHUNKS[step + 1]):
                size = R // CHUNKS[step + 1]
                g_vec[step + 1][ch][own + half] = rounded[ch * size:(ch + 1) * size]
            q = nugget * p_own + rounded.astype(jnp.float32)
            pq, rq, qq = pq + p_own * q, rq + r_own * q, qq + q * q
            rr = rr + r_own * r_own
        rows = [as_lanes(a) for a in ((pq, rq, qq, rr) if step == 0 else (pq, rq, qq))]
        ar = sum_start(step, rows)
        if step < 2:
            halo = halo_start(h_vec.at[step + 1])
        if step == 2:
            outward.append(Journey(3, 1))
        if step > 0:
            outward[step - 1].forward()
        if step == 2:
            outward[1].column()
        ar = sum_second(step, ar)
        if step == 1:
            outward[0].column()
        if step < 2:
            outward.append(Journey(step + 1, 1))
        else:
            outward[2].through()
        totals = sum_finish(step, ar)
        if step == 0:
            norm_now = totals[3:4]
        alpha = norm_now / totals[0:1]
        coef[2 * step] = as_rows(alpha)
        if step < 2:
            norm_next = norm_now - 2.0 * alpha * totals[1:2] + alpha * alpha * totals[2:3]
            norm_next = jnp.maximum(norm_next, 0.0)
            coef[2 * step + 1] = as_rows(norm_next / norm_now)
            norm_now = norm_next

    images = [outward[step].sums(0) for step in range(2)]
    for ch in range(CHUNKS[3]):
        last = outward[2].sums(ch)
        rows = rows_of(3, ch)
        size = R // CHUNKS[3]
        cut = slice(ch * size, (ch + 1) * size)
        for half in range(2):
            lanes = pl.ds(half * BLOCK, BLOCK)
            residual = direction = right_ref[rows, lanes]
            total = jnp.zeros_like(residual)
            for step in range(3):
                image = last[half] if step == 2 else images[step][half][cut]
                total = total + coef[2 * step, rows, :] * direction
                residual = residual - coef[2 * step, rows, :] * (nugget * direction + image)
                if step < 2:
                    direction = residual + coef[2 * step + 1, rows, :] * direction
            solution_ref[rows, lanes] = total
            residual_ref[rows, lanes] = residual

    assert len(phases) == PHASES
    for phase, view in enumerate(phases):
        pltpu.make_async_copy(view, view, send.at[phase]).wait()


def per_device(side, depth, point_data, right_side, pair_list):
    R = right_side.shape[0]
    chips = side * side
    f32, bf16 = jnp.float32, jnp.bfloat16
    vmem = pl.BlockSpec(memory_space=pltpu.VMEM)
    out = jax.ShapeDtypeStruct(right_side.shape, f32)
    return pl.pallas_call(
        functools.partial(kernel, side, depth),
        out_shape=(out, out),
        in_specs=[pl.BlockSpec(memory_space=pltpu.HBM)] * 2,
        out_specs=(vmem, vmem),
        scratch_shapes=[
            *[pltpu.VMEM((4 * chips + 1, R // n, BLOCK), bf16) for n in CHUNKS for _ in range(n)],
            *[pltpu.VMEM((n, 2 * depth, R // n, BLOCK), bf16) for n in CHUNKS],
            *[pltpu.VMEM((n, 2 * depth, R // n, BLOCK), bf16) for n in CHUNKS],
            pltpu.VMEM((4 * chips + 1, 8, BLOCK), f32),
            pltpu.VMEM((2 * depth, 8, BLOCK), f32),
            pltpu.VMEM((2 * depth, 8, BLOCK), f32),
            pltpu.VMEM((2 * depth, 8, BLOCK), f32),
            pltpu.VMEM((36, 8, BLOCK), f32),
            pltpu.VMEM((3, 36, R, BLOCK), bf16),
            pltpu.VMEM((9, 4 * BLOCK, 2 * BLOCK), bf16),
            pltpu.VMEM((36, R, BLOCK), f32),
            pltpu.VMEM((36, R, BLOCK), f32),
            pltpu.VMEM((3, chips, 4, BLOCK), f32),
            pltpu.VMEM((3, 2 * depth, 4, BLOCK), f32),
            pltpu.VMEM((2, 8, BLOCK), jnp.int32),
            pltpu.SMEM((2, 8, BLOCK), jnp.int32),
            pltpu.VMEM((6, R, BLOCK), f32),
            pltpu.VMEM(point_data.shape, f32),
            pltpu.VMEM(right_side.shape, f32),
            pltpu.SemaphoreType.DMA((PHASES,)),
            pltpu.SemaphoreType.DMA((PHASES,)),
            pltpu.SemaphoreType.DMA((2,)),
        ],
        compiler_params=pltpu.CompilerParams(
            collective_id=0, has_side_effects=True, vmem_limit_bytes=40 << 20
        ),
    )(point_data, right_side)


def build(mesh, side):
    depth = mesh.shape["row"]
    placed = P(None, ("row", "col"))
    return jax.shard_map(
        functools.partial(per_device, side, depth),
        mesh=mesh,
        in_specs=(placed, placed, P()),
        out_specs=(placed, placed),
        check_vma=False,
    )


def solution(mesh):
    return build(mesh, SIDE)
```

```python
import functools

import jax
import jax.numpy as jnp
from jax import lax
from jax.experimental import pallas as pl
from jax.experimental.pallas import tpu as pltpu
from jax.sharding import PartitionSpec as P

SIDE = 4
BLOCK = 128
MESH = pl.DeviceIdType.MESH
long_range = 1.0
short_range = 0.35
nugget = 1.0
CHUNKS = (4, 1, 1, 4)
PHASES = 14 + 3 * sum(CHUNKS)


def covariance(xj, yj, zj, sj, xi, yi, zi, si):
    dx, dy, dz = xj - xi, yj - yi, zj - zi
    d = jnp.sqrt(dx * dx + dy * dy + dz * dz)

    def wendland(u):
        remain = jnp.maximum(1.0 - u, 0.0)
        square = remain * remain
        return square * square * (4.0 * u + 1.0)

    return sj * (wendland(d * (1.0 / long_range)) + wendland(d * (1.0 / short_range))) * si


def kernel(side, depth, point_hbm, right_hbm, solution_ref, residual_ref, *scratch):
    chips = side * side
    slots = 4 * chips
    zslots = 2 * depth
    R = right_hbm.shape[0]
    g_vec = [list(scratch[sum(CHUNKS[:v]):sum(CHUNKS[:v + 1])]) for v in range(4)]
    zs_vec = scratch[sum(CHUNKS):sum(CHUNKS) + 4]
    zr_vec = scratch[sum(CHUNKS) + 4:sum(CHUNKS) + 8]
    (g_pts, line_pts, zs_pts, zr_pts, h_pts, h_vec, tiles, p_all, r_all, ar_one, ar_two,
     table_v, table_s, coef, point_ref, right_ref, send, recv, local_sem) = scratch[sum(CHUNKS) + 8:]
    my_z = lax.axis_index("row")
    my_col = lax.axis_index("col")
    core = my_col % 2
    chip = my_col // 2
    xx = chip % side
    yy = chip // side
    zs = my_z * 2 + core
    own = (core * chips + chip) * 2
    sibling = (my_z, chip * 2 + 1 - core)

    def rows_of(v, ch):
        size = R // CHUNKS[v]
        return pl.ds(ch * size, size)

    def device(zslot, chip_):
        return (zslot // 2, chip_ * 2 + zslot % 2)

    def shifted(ox, oy):
        return ((yy + oy) % side) * side + (xx + ox) % side

    def plane_peer(o):
        return device(zs, shifted(o % side, o // side))

    def line_peer(o):
        return device((my_z + o) % depth * 2 + core, chip)

    def pillar_peer(o):
        return device((zs + o) % zslots, chip)

    def neighbour(n, oz):
        return device((zs + oz + zslots) % zslots, shifted(n // 3 - 1 + side, n % 3 - 1 + side))

    def push(src, dst, phase, peer):
        pltpu.make_async_remote_copy(
            src_ref=src, dst_ref=dst, send_sem=send.at[phase], recv_sem=recv.at[phase],
            device_id=peer, device_id_type=MESH,
        ).start()

    phases = []

    def new_phase(view):
        phases.append(view)
        return len(phases) - 1

    def arrived(phase):
        view = phases[phase]
        pltpu.make_async_copy(view, view, recv.at[phase]).wait()

    def loop(lo, hi, body):
        lax.fori_loop(lo, hi, lambda i, c: (body(i), c)[1], 0)

    def plane_start(buf):
        phase = new_phase(buf.at[pl.ds(0, 2 * (chips - 1))])
        part = buf.at[pl.ds(own, 2)]
        loop(1, chips, lambda o: push(part, part, phase, plane_peer(o)))
        return phase

    def forward_start(buf):
        phase = new_phase(buf.at[pl.ds(0, 2 * chips)])
        part = buf.at[pl.ds(core * 2 * chips, 2 * chips)]
        push(part, part, phase, sibling)
        return phase

    def column_start(buf, staged, into, table):
        phase = new_phase(into.at[pl.ds(0, 2 * (depth - 1))])
        for t in range(2 * depth):
            staged[t] = buf[table_s[table, 4, t]]
        into[2 * my_z] = staged[2 * my_z]
        into[2 * my_z + 1] = staged[2 * my_z + 1]

        def one(o):
            z_to = (my_z + o) % depth
            push(staged.at[pl.ds(2 * z_to, 2)], into.at[pl.ds(2 * my_z, 2)], phase, line_peer(o))

        loop(1, depth, one)
        return phase

    def column_sum(into):
        pair = []
        for half in range(2):
            total = into[half].astype(jnp.float32)
            for z in range(1, depth):
                total = total + into[2 * z + half].astype(jnp.float32)
            pair.append(total)
        return pair

    def halo_start(buf):
        phase = new_phase(buf.at[pl.ds(0, 34)])

        def one(n):
            there = (8 - n) * 4

            @pl.when(n != 4)
            def _():
                push(buf.at[pl.ds(17, 2)], buf.at[pl.ds(there + 1, 2)], phase, neighbour(n, 0))

            push(buf.at[pl.ds(18, 1)], buf.at[pl.ds(there, 1)], phase, neighbour(n, 1))
            push(buf.at[pl.ds(17, 1)], buf.at[pl.ds(there + 3, 1)], phase, neighbour(n, -1))

        loop(0, 9, one)
        return phase

    class Journey:
        def __init__(self, v, table):
            self.v, self.table, self.count = v, table, CHUNKS[v]
            self.planes = [plane_start(buf) for buf in g_vec[v]]
            self.forwards, self.columns = [], []

        def forward(self):
            ch = len(self.forwards)
            arrived(self.planes[ch])
            self.forwards.append(forward_start(g_vec[self.v][ch]))

        def column(self):
            ch = len(self.columns)
            arrived(self.forwards[ch])
            self.columns.append(column_start(
                g_vec[self.v][ch], zs_vec[self.v].at[ch], zr_vec[self.v].at[ch], self.table))

        def through(self):
            self.forward()
            for _ in range(1, self.count):
                self.forward()
                self.column()
            self.column()

        def sums(self, ch):
            arrived(self.columns[ch])
            return column_sum(zr_vec[self.v].at[ch])

    load = [
        pltpu.make_async_copy(point_hbm, point_ref, local_sem.at[0]),
        pltpu.make_async_copy(right_hbm, right_ref, local_sem.at[1]),
    ]
    for copy in load:
        copy.start()

    barrier = pltpu.get_barrier_semaphore()

    def greet(peer):
        pl.semaphore_signal(barrier, inc=1, device_id=peer, device_id_type=MESH)

    loop(1, chips, lambda o: greet(plane_peer(o)))
    loop(1, depth, lambda o: greet(line_peer(o)))
    greet(sibling)
    load[0].wait()
    pts = point_ref[...]
    for half in range(2):
        here = pts[:, half * BLOCK:(half + 1) * BLOCK]
        low = jnp.broadcast_to(jnp.floor(jnp.min(here, axis=1, keepdims=True)), (4, BLOCK))
        cx = jnp.clip(low[0:1], 0.0, side - 1.0)
        cy = jnp.clip(low[1:2], 0.0, side - 1.0)
        cz = jnp.clip(low[2:3], 0.0, 4.0 * depth - 1.0)
        slab = jnp.floor(cz * 0.25)
        level = cz - 4.0 * slab
        upper = jnp.floor(level * 0.5)
        slot = (upper * chips + cy * side + cx) * 2.0 + (level - 2.0 * upper)
        g_pts[own + half] = jnp.zeros((8, BLOCK), jnp.float32)
        g_pts[own + half, 0:4, :] = here
        g_pts[own + half, 4:5, :] = slab * slots + slot
        g_pts[own + half, 5:6, :] = slot
        g_pts[own + half, 6:7, :] = slab
        line_pts[2 * my_z + half] = g_pts[own + half]
    load[1].wait()
    for half in range(2):
        for ch in range(CHUNKS[0]):
            part = right_ref[rows_of(0, ch), half * BLOCK:(half + 1) * BLOCK]
            g_vec[0][ch][own + half] = part.astype(jnp.bfloat16)
    g_pts[slots] = jnp.zeros((8, BLOCK), jnp.float32)
    for v in range(4):
        for buf in g_vec[v]:
            buf[slots] = jnp.zeros((R // CHUNKS[v], BLOCK), jnp.bfloat16)

    pl.semaphore_wait(barrier, chips - 1 + depth - 1 + 1)

    pts_plane = plane_start(g_pts)
    line = new_phase(line_pts.at[pl.ds(0, 2 * (depth - 1))])
    mine = line_pts.at[pl.ds(2 * my_z, 2)]
    loop(1, depth, lambda o: push(mine, mine, line, line_peer(o)))
    inward = Journey(0, 0)
    arrived(pts_plane)
    pts_forward = forward_start(g_pts)
    arrived(line)

    lane = lax.broadcasted_iota(jnp.int32, (8, BLOCK), 1)
    target = ((lane // 2) * slots + (own + lane % 2)).astype(jnp.float32)
    gap = jnp.float32(slots)
    slab_here = lax.convert_element_type(my_z, jnp.float32)
    acc = jnp.full((8, BLOCK), gap, jnp.float32)
    for t in range(2 * depth):
        tile = line_pts[t]
        value = jnp.where(tile[6:7] == slab_here, tile[5:6], gap)
        acc = jnp.where(lane == t, jnp.broadcast_to(value, (8, BLOCK)), acc)
    table_v[1] = jnp.clip(acc.astype(jnp.int32), 0, slots)

    arrived(pts_forward)
    acc = jnp.full((8, BLOCK), gap, jnp.float32)
    for k in range(slots):
        acc = jnp.minimum(acc, jnp.where(g_pts[k] == target, jnp.float32(k), gap))
    table_v[0] = jnp.clip(acc.astype(jnp.int32), 0, slots)
    copy = pltpu.make_async_copy(table_v, table_s, local_sem.at[0])
    copy.start()
    copy.wait()

    pts_column = column_start(g_pts, zs_pts, zr_pts, 0)
    inward.through()
    arrived(pts_column)
    for half, total in enumerate(column_sum(zr_pts)):
        h_pts[17 + half] = total
    pts_halo = halo_start(h_pts)
    for ch in range(CHUNKS[0]):
        for half, total in enumerate(inward.sums(ch)):
            h_vec[0, 17 + half, rows_of(0, ch), :] = total.astype(jnp.bfloat16)
    halo = halo_start(h_vec.at[0])

    arrived(pts_halo)

    def tile_column(n):
        for level in range(4):
            other = jnp.transpose(h_pts[n * 4 + level])
            xj, yj, zj, sj = (other[:, a:a + 1] for a in range(4))
            for half in range(2):
                rows, lanes = pl.ds(level * BLOCK, BLOCK), pl.ds(half * BLOCK, BLOCK)
                if not 0 <= level - half <= 2:
                    tiles[n, rows, lanes] = jnp.zeros((BLOCK, BLOCK), jnp.bfloat16)
                    continue
                xi, yi, zi, si = (h_pts[17 + half, a:a + 1, :] for a in range(4))
                tiles[n, rows, lanes] = covariance(xj, yj, zj, sj, xi, yi, zi, si).astype(jnp.bfloat16)

    loop(0, 9, tile_column)

    eye = lax.broadcasted_iota(jnp.int32, (R, BLOCK), 0) == lax.broadcasted_iota(jnp.int32, (R, BLOCK), 1)
    row4 = lax.broadcasted_iota(jnp.int32, (4, BLOCK), 0)

    def as_lanes(values):
        total = jnp.sum(values, axis=1, keepdims=True)
        return jnp.sum(jnp.where(eye, total, 0.0), axis=0, keepdims=True)

    def as_rows(values):
        column = jnp.sum(jnp.where(eye, values, 0.0), axis=1, keepdims=True)
        return jnp.broadcast_to(column, (R, BLOCK))

    def sum_start(step, rows):
        tile = jnp.zeros((4, BLOCK), jnp.float32)
        for i, value in enumerate(rows):
            tile = jnp.where(row4 == i, value, tile)
        buf = ar_one.at[step]
        buf[chip] = tile
        phase = new_phase(buf.at[pl.ds(0, chips - 1)])
        part = buf.at[pl.ds(chip, 1)]
        loop(1, chips, lambda o: push(part, part, phase, plane_peer(o)))
        return phase

    def sum_second(step, phase):
        arrived(phase)
        buf, second = ar_one.at[step], ar_two.at[step]
        total = buf[0]
        for i in range(1, chips):
            total = total + buf[i]
        second[zs] = total
        phase = new_phase(second.at[pl.ds(0, zslots - 1)])
        part = second.at[pl.ds(zs, 1)]
        loop(1, zslots, lambda o: push(part, part, phase, pillar_peer(o)))
        return phase

    def sum_finish(step, phase):
        arrived(phase)
        second = ar_two.at[step]
        total = second[0]
        for i in range(1, zslots):
            total = total + second[i]
        return total

    outward = []
    norm_now = None
    for step in range(3):
        arrived(halo)
        product = jnp.zeros((R, 2 * BLOCK), jnp.float32)
        for n in range(9):
            parts = []
            for level in range(4):
                k = n * 4 + level
                if step == 0:
                    parts.append(h_vec[0, k])
                    continue
                if step == 1:
                    p_old = h_vec[0, k].astype(jnp.float32)
                    r_old = p_old
                else:
                    p_old, r_old = p_all[k], r_all[k]
                image = nugget * p_old + h_vec[step, k].astype(jnp.float32)
                r_new = r_old - coef[2 * step - 2] * image
                p_new = r_new + coef[2 * step - 1] * p_old
                r_all[k] = r_new
                p_all[k] = p_new
                parts.append(p_new.astype(jnp.bfloat16))
            lhs = jnp.concatenate(parts, axis=1)
            product = product + jnp.dot(lhs, tiles[n], preferred_element_type=jnp.float32)
        pq = rq = qq = rr = jnp.zeros((R, BLOCK), jnp.float32)
        for half in range(2):
            if step == 0:
                p_own = h_vec[0, 17 + half].astype(jnp.float32)
                r_own = p_own
            else:
                p_own, r_own = p_all[17 + half], r_all[17 + half]
            rounded = product[:, half * BLOCK:(half + 1) * BLOCK].astype(jnp.bfloat16)
            if step < 2:
                h_vec[step + 1, 17 + half] = rounded
            for ch in range(CHUNKS[step + 1]):
                size = R // CHUNKS[step + 1]
                g_vec[step + 1][ch][own + half] = rounded[ch * size:(ch + 1) * size]
            q = nugget * p_own + rounded.astype(jnp.float32)
            pq, rq, qq = pq + p_own * q, rq + r_own * q, qq + q * q
            rr = rr + r_own * r_own
        rows = [as_lanes(a) for a in ((pq, rq, qq, rr) if step == 0 else (pq, rq, qq))]
        ar = sum_start(step, rows)
        if step < 2:
            halo = halo_start(h_vec.at[step + 1])
        if step == 2:
            outward.append(Journey(3, 1))
        if step > 0:
            outward[step - 1].forward()
        ar = sum_second(step, ar)
        if step > 0:
            outward[step - 1].column()
        if step < 2:
            outward.append(Journey(step + 1, 1))
        else:
            outward[2].through()
        totals = sum_finish(step, ar)
        if step == 0:
            norm_now = totals[3:4]
        alpha = norm_now / totals[0:1]
        coef[2 * step] = as_rows(alpha)
        if step < 2:
            norm_next = norm_now - 2.0 * alpha * totals[1:2] + alpha * alpha * totals[2:3]
            norm_next = jnp.maximum(norm_next, 0.0)
            coef[2 * step + 1] = as_rows(norm_next / norm_now)
            norm_now = norm_next

    images = [outward[step].sums(0) for step in range(2)]
    for ch in range(CHUNKS[3]):
        last = outward[2].sums(ch)
        rows = rows_of(3, ch)
        size = R // CHUNKS[3]
        cut = slice(ch * size, (ch + 1) * size)
        for half in range(2):
            lanes = pl.ds(half * BLOCK, BLOCK)
            residual = direction = right_ref[rows, lanes]
            total = jnp.zeros_like(residual)
            for step in range(3):
                image = last[half] if step == 2 else images[step][half][cut]
                total = total + coef[2 * step, rows, :] * direction
                residual = residual - coef[2 * step, rows, :] * (nugget * direction + image)
                if step < 2:
                    direction = residual + coef[2 * step + 1, rows, :] * direction
            solution_ref[rows, lanes] = total
            residual_ref[rows, lanes] = residual

    assert len(phases) == PHASES
    for phase, view in enumerate(phases):
        pltpu.make_async_copy(view, view, send.at[phase]).wait()


def per_device(side, depth, point_data, right_side, pair_list):
    R = right_side.shape[0]
    chips = side * side
    f32, bf16 = jnp.float32, jnp.bfloat16
    vmem = pl.BlockSpec(memory_space=pltpu.VMEM)
    out = jax.ShapeDtypeStruct(right_side.shape, f32)
    return pl.pallas_call(
        functools.partial(kernel, side, depth),
        out_shape=(out, out),
        in_specs=[pl.BlockSpec(memory_space=pltpu.HBM)] * 2,
        out_specs=(vmem, vmem),
        scratch_shapes=[
            *[pltpu.VMEM((4 * chips + 1, R // n, BLOCK), bf16) for n in CHUNKS for _ in range(n)],
            *[pltpu.VMEM((n, 2 * depth, R // n, BLOCK), bf16) for n in CHUNKS],
            *[pltpu.VMEM((n, 2 * depth, R // n, BLOCK), bf16) for n in CHUNKS],
            pltpu.VMEM((4 * chips + 1, 8, BLOCK), f32),
            pltpu.VMEM((2 * depth, 8, BLOCK), f32),
            pltpu.VMEM((2 * depth, 8, BLOCK), f32),
            pltpu.VMEM((2 * depth, 8, BLOCK), f32),
            pltpu.VMEM((36, 8, BLOCK), f32),
            pltpu.VMEM((3, 36, R, BLOCK), bf16),
            pltpu.VMEM((9, 4 * BLOCK, 2 * BLOCK), bf16),
            pltpu.VMEM((36, R, BLOCK), f32),
            pltpu.VMEM((36, R, BLOCK), f32),
            pltpu.VMEM((3, chips, 4, BLOCK), f32),
            pltpu.VMEM((3, 2 * depth, 4, BLOCK), f32),
            pltpu.VMEM((2, 8, BLOCK), jnp.int32),
            pltpu.SMEM((2, 8, BLOCK), jnp.int32),
            pltpu.VMEM((6, R, BLOCK), f32),
            pltpu.VMEM(point_data.shape, f32),
            pltpu.VMEM(right_side.shape, f32),
            pltpu.SemaphoreType.DMA((PHASES,)),
            pltpu.SemaphoreType.DMA((PHASES,)),
            pltpu.SemaphoreType.DMA((2,)),
        ],
        compiler_params=pltpu.CompilerParams(
            collective_id=0, has_side_effects=True, vmem_limit_bytes=40 << 20
        ),
    )(point_data, right_side)


def build(mesh, side):
    depth = mesh.shape["row"]
    placed = P(None, ("row", "col"))
    return jax.shard_map(
        functools.partial(per_device, side, depth),
        mesh=mesh,
        in_specs=(placed, placed, P()),
        out_specs=(placed, placed),
        check_vma=False,
    )


def solution(mesh):
    return build(mesh, SIDE)
```

```python
import functools

import jax
import jax.numpy as jnp
from jax import lax
from jax.experimental import pallas as pl
from jax.experimental.pallas import tpu as pltpu
from jax.sharding import PartitionSpec as P

SIDE = 4
BLOCK = 128
MESH = pl.DeviceIdType.MESH
long_range = 1.0
short_range = 0.35
nugget = 1.0
CHUNKS = (4, 1, 1, 4)
PHASES = 14 + 3 * sum(CHUNKS)


def covariance(xj, yj, zj, sj, xi, yi, zi, si):
    dx, dy, dz = xj - xi, yj - yi, zj - zi
    d = jnp.sqrt(dx * dx + dy * dy + dz * dz)

    def wendland(u):
        remain = jnp.maximum(1.0 - u, 0.0)
        square = remain * remain
        return square * square * (4.0 * u + 1.0)

    return sj * (wendland(d * (1.0 / long_range)) + wendland(d * (1.0 / short_range))) * si


def kernel(side, depth, point_hbm, right_hbm, solution_ref, residual_ref, *scratch):
    chips = side * side
    slots = 4 * chips
    zslots = 2 * depth
    R = right_hbm.shape[0]
    g_vec = [list(scratch[sum(CHUNKS[:v]):sum(CHUNKS[:v + 1])]) for v in range(4)]
    zs_vec = scratch[sum(CHUNKS):sum(CHUNKS) + 4]
    zr_vec = scratch[sum(CHUNKS) + 4:sum(CHUNKS) + 8]
    (g_pts, line_pts, zs_pts, zr_pts, h_pts, h_vec, tiles, p_all, r_all, ar_one, ar_two,
     table_v, table_s, coef, point_ref, right_ref, send, recv, local_sem) = scratch[sum(CHUNKS) + 8:]
    my_z = lax.axis_index("row")
    my_col = lax.axis_index("col")
    core = my_col % 2
    chip = my_col // 2
    xx = chip % side
    yy = chip // side
    zs = my_z * 2 + core
    own = (core * chips + chip) * 2
    sibling = (my_z, chip * 2 + 1 - core)

    def rows_of(v, ch):
        size = R // CHUNKS[v]
        return pl.ds(ch * size, size)

    def device(zslot, chip_):
        return (zslot // 2, chip_ * 2 + zslot % 2)

    def shifted(ox, oy):
        return ((yy + oy) % side) * side + (xx + ox) % side

    def plane_peer(o):
        return device(zs, shifted(o % side, o // side))

    def line_peer(o):
        return device((my_z + o) % depth * 2 + core, chip)

    def pillar_peer(o):
        return device((zs + o) % zslots, chip)

    def neighbour(n, oz):
        return device((zs + oz + zslots) % zslots, shifted(n // 3 - 1 + side, n % 3 - 1 + side))

    def push(src, dst, phase, peer):
        pltpu.make_async_remote_copy(
            src_ref=src, dst_ref=dst, send_sem=send.at[phase], recv_sem=recv.at[phase],
            device_id=peer, device_id_type=MESH,
        ).start()

    phases = []

    def new_phase(view):
        phases.append(view)
        return len(phases) - 1

    def arrived(phase):
        view = phases[phase]
        pltpu.make_async_copy(view, view, recv.at[phase]).wait()

    def loop(lo, hi, body):
        lax.fori_loop(lo, hi, lambda i, c: (body(i), c)[1], 0)

    def plane_start(buf):
        phase = new_phase(buf.at[pl.ds(0, 2 * (chips - 1))])
        part = buf.at[pl.ds(own, 2)]
        loop(1, chips, lambda o: push(part, part, phase, plane_peer(o)))
        return phase

    def forward_start(buf):
        phase = new_phase(buf.at[pl.ds(0, 2 * chips)])
        part = buf.at[pl.ds(core * 2 * chips, 2 * chips)]
        push(part, part, phase, sibling)
        return phase

    def column_start(buf, staged, into, table):
        phase = new_phase(into.at[pl.ds(0, 2 * (depth - 1))])
        for t in range(2 * depth):
            staged[t] = buf[table_s[table, 4, t]]
        into[2 * my_z] = staged[2 * my_z]
        into[2 * my_z + 1] = staged[2 * my_z + 1]

        def one(o):
            z_to = (my_z + o) % depth
            push(staged.at[pl.ds(2 * z_to, 2)], into.at[pl.ds(2 * my_z, 2)], phase, line_peer(o))

        loop(1, depth, one)
        return phase

    def column_sum(into):
        pair = []
        for half in range(2):
            total = into[half].astype(jnp.float32)
            for z in range(1, depth):
                total = total + into[2 * z + half].astype(jnp.float32)
            pair.append(total)
        return pair

    def halo_start(buf):
        phase = new_phase(buf.at[pl.ds(0, 34)])

        def one(n):
            there = (8 - n) * 4

            @pl.when(n != 4)
            def _():
                push(buf.at[pl.ds(17, 2)], buf.at[pl.ds(there + 1, 2)], phase, neighbour(n, 0))

            push(buf.at[pl.ds(18, 1)], buf.at[pl.ds(there, 1)], phase, neighbour(n, 1))
            push(buf.at[pl.ds(17, 1)], buf.at[pl.ds(there + 3, 1)], phase, neighbour(n, -1))

        loop(0, 9, one)
        return phase

    class Journey:
        def __init__(self, v, table):
            self.v, self.table, self.count = v, table, CHUNKS[v]
            self.planes = [plane_start(buf) for buf in g_vec[v]]
            self.forwards, self.columns = [], []

        def forward(self):
            ch = len(self.forwards)
            arrived(self.planes[ch])
            self.forwards.append(forward_start(g_vec[self.v][ch]))

        def column(self):
            ch = len(self.columns)
            arrived(self.forwards[ch])
            self.columns.append(column_start(
                g_vec[self.v][ch], zs_vec[self.v].at[ch], zr_vec[self.v].at[ch], self.table))

        def through(self):
            self.forward()
            for _ in range(1, self.count):
                self.forward()
                self.column()
            self.column()

        def sums(self, ch):
            arrived(self.columns[ch])
            return column_sum(zr_vec[self.v].at[ch])

    load = [
        pltpu.make_async_copy(point_hbm, point_ref, local_sem.at[0]),
        pltpu.make_async_copy(right_hbm, right_ref, local_sem.at[1]),
    ]
    for copy in load:
        copy.start()

    barrier = pltpu.get_barrier_semaphore()

    def greet(peer):
        pl.semaphore_signal(barrier, inc=1, device_id=peer, device_id_type=MESH)

    loop(1, chips, lambda o: greet(plane_peer(o)))
    loop(1, depth, lambda o: greet(line_peer(o)))
    greet(sibling)
    load[0].wait()
    pts = point_ref[...]
    for half in range(2):
        here = pts[:, half * BLOCK:(half + 1) * BLOCK]
        low = jnp.broadcast_to(jnp.floor(jnp.min(here, axis=1, keepdims=True)), (4, BLOCK))
        cx = jnp.clip(low[0:1], 0.0, side - 1.0)
        cy = jnp.clip(low[1:2], 0.0, side - 1.0)
        cz = jnp.clip(low[2:3], 0.0, 4.0 * depth - 1.0)
        slab = jnp.floor(cz * 0.25)
        level = cz - 4.0 * slab
        upper = jnp.floor(level * 0.5)
        slot = (upper * chips + cy * side + cx) * 2.0 + (level - 2.0 * upper)
        g_pts[own + half] = jnp.zeros((8, BLOCK), jnp.float32)
        g_pts[own + half, 0:4, :] = here
        g_pts[own + half, 4:5, :] = slab * slots + slot
        g_pts[own + half, 5:6, :] = slot
        g_pts[own + half, 6:7, :] = slab
        line_pts[2 * my_z + half] = g_pts[own + half]
    load[1].wait()
    for half in range(2):
        for ch in range(CHUNKS[0]):
            part = right_ref[rows_of(0, ch), half * BLOCK:(half + 1) * BLOCK]
            g_vec[0][ch][own + half] = part.astype(jnp.bfloat16)
    g_pts[slots] = jnp.zeros((8, BLOCK), jnp.float32)
    for v in range(4):
        for buf in g_vec[v]:
            buf[slots] = jnp.zeros((R // CHUNKS[v], BLOCK), jnp.bfloat16)

    pl.semaphore_wait(barrier, chips - 1 + depth - 1 + 1)

    pts_plane = plane_start(g_pts)
    line = new_phase(line_pts.at[pl.ds(0, 2 * (depth - 1))])
    mine = line_pts.at[pl.ds(2 * my_z, 2)]
    loop(1, depth, lambda o: push(mine, mine, line, line_peer(o)))
    inward = Journey(0, 0)
    arrived(pts_plane)
    pts_forward = forward_start(g_pts)
    arrived(line)

    lane = lax.broadcasted_iota(jnp.int32, (8, BLOCK), 1)
    target = ((lane // 2) * slots + (own + lane % 2)).astype(jnp.float32)
    gap = jnp.float32(slots)
    slab_here = lax.convert_element_type(my_z, jnp.float32)
    acc = jnp.full((8, BLOCK), gap, jnp.float32)
    for t in range(2 * depth):
        tile = line_pts[t]
        value = jnp.where(tile[6:7] == slab_here, tile[5:6], gap)
        acc = jnp.where(lane == t, jnp.broadcast_to(value, (8, BLOCK)), acc)
    table_v[1] = jnp.clip(acc.astype(jnp.int32), 0, slots)

    arrived(pts_forward)
    acc = jnp.full((8, BLOCK), gap, jnp.float32)
    for k in range(slots):
        acc = jnp.minimum(acc, jnp.where(g_pts[k] == target, jnp.float32(k), gap))
    table_v[0] = jnp.clip(acc.astype(jnp.int32), 0, slots)
    copy = pltpu.make_async_copy(table_v, table_s, local_sem.at[0])
    copy.start()
    copy.wait()

    pts_column = column_start(g_pts, zs_pts, zr_pts, 0)
    inward.through()
    arrived(pts_column)
    for half, total in enumerate(column_sum(zr_pts)):
        h_pts[17 + half] = total
    pts_halo = halo_start(h_pts)
    for ch in range(CHUNKS[0]):
        for half, total in enumerate(inward.sums(ch)):
            h_vec[0, 17 + half, rows_of(0, ch), :] = total.astype(jnp.bfloat16)
    halo = halo_start(h_vec.at[0])

    arrived(pts_halo)

    def tile_column(n):
        for level in range(4):
            other = jnp.transpose(h_pts[n * 4 + level])
            xj, yj, zj, sj = (other[:, a:a + 1] for a in range(4))
            for half in range(2):
                rows, lanes = pl.ds(level * BLOCK, BLOCK), pl.ds(half * BLOCK, BLOCK)
                if not 0 <= level - half <= 2:
                    tiles[n, rows, lanes] = jnp.zeros((BLOCK, BLOCK), jnp.bfloat16)
                    continue
                xi, yi, zi, si = (h_pts[17 + half, a:a + 1, :] for a in range(4))
                tiles[n, rows, lanes] = covariance(xj, yj, zj, sj, xi, yi, zi, si).astype(jnp.bfloat16)

    loop(0, 9, tile_column)

    eye = lax.broadcasted_iota(jnp.int32, (R, BLOCK), 0) == lax.broadcasted_iota(jnp.int32, (R, BLOCK), 1)
    row4 = lax.broadcasted_iota(jnp.int32, (4, BLOCK), 0)

    def as_lanes(values):
        total = jnp.sum(values, axis=1, keepdims=True)
        return jnp.sum(jnp.where(eye, total, 0.0), axis=0, keepdims=True)

    def as_rows(values):
        column = jnp.sum(jnp.where(eye, values, 0.0), axis=1, keepdims=True)
        return jnp.broadcast_to(column, (R, BLOCK))

    def sum_start(step, rows):
        tile = jnp.zeros((4, BLOCK), jnp.float32)
        for i, value in enumerate(rows):
            tile = jnp.where(row4 == i, value, tile)
        buf = ar_one.at[step]
        buf[chip] = tile
        phase = new_phase(buf.at[pl.ds(0, chips - 1)])
        part = buf.at[pl.ds(chip, 1)]
        loop(1, chips, lambda o: push(part, part, phase, plane_peer(o)))
        return phase

    def sum_second(step, phase):
        arrived(phase)
        buf, second = ar_one.at[step], ar_two.at[step]
        total = buf[0]
        for i in range(1, chips):
            total = total + buf[i]
        second[zs] = total
        phase = new_phase(second.at[pl.ds(0, zslots - 1)])
        part = second.at[pl.ds(zs, 1)]
        loop(1, zslots, lambda o: push(part, part, phase, pillar_peer(o)))
        return phase

    def sum_finish(step, phase):
        arrived(phase)
        second = ar_two.at[step]
        total = second[0]
        for i in range(1, zslots):
            total = total + second[i]
        return total

    outward = []
    norm_now = None
    for step in range(3):
        arrived(halo)
        product = jnp.zeros((R, 2 * BLOCK), jnp.float32)
        for n in range(9):
            parts = []
            for level in range(4):
                k = n * 4 + level
                if step == 0:
                    parts.append(h_vec[0, k])
                    continue
                if step == 1:
                    p_old = h_vec[0, k].astype(jnp.float32)
                    r_old = p_old
                else:
                    p_old, r_old = p_all[k], r_all[k]
                image = nugget * p_old + h_vec[step, k].astype(jnp.float32)
                r_new = r_old - coef[2 * step - 2] * image
                p_new = r_new + coef[2 * step - 1] * p_old
                r_all[k] = r_new
                p_all[k] = p_new
                parts.append(p_new.astype(jnp.bfloat16))
            lhs = jnp.concatenate(parts, axis=1)
            product = product + jnp.dot(lhs, tiles[n], preferred_element_type=jnp.float32)
        pq = rq = qq = rr = jnp.zeros((R, BLOCK), jnp.float32)
        for half in range(2):
            if step == 0:
                p_own = h_vec[0, 17 + half].astype(jnp.float32)
                r_own = p_own
            else:
                p_own, r_own = p_all[17 + half], r_all[17 + half]
            rounded = product[:, half * BLOCK:(half + 1) * BLOCK].astype(jnp.bfloat16)
            if step < 2:
                h_vec[step + 1, 17 + half] = rounded
            for ch in range(CHUNKS[step + 1]):
                size = R // CHUNKS[step + 1]
                g_vec[step + 1][ch][own + half] = rounded[ch * size:(ch + 1) * size]
            q = nugget * p_own + rounded.astype(jnp.float32)
            pq, rq, qq = pq + p_own * q, rq + r_own * q, qq + q * q
            rr = rr + r_own * r_own
        rows = [as_lanes(a) for a in ((pq, rq, qq, rr) if step == 0 else (pq, rq, qq))]
        ar = sum_start(step, rows)
        if step < 2:
            halo = halo_start(h_vec.at[step + 1])
        if step == 2:
            outward.append(Journey(3, 1))
        if step > 0:
            outward[step - 1].forward()
        ar = sum_second(step, ar)
        if step > 0:
            outward[step - 1].column()
        if step < 2:
            outward.append(Journey(step + 1, 1))
        else:
            outward[2].through()
        totals = sum_finish(step, ar)
        if step == 0:
            norm_now = totals[3:4]
        alpha = norm_now / totals[0:1]
        coef[2 * step] = as_rows(alpha)
        if step < 2:
            norm_next = norm_now - 2.0 * alpha * totals[1:2] + alpha * alpha * totals[2:3]
            norm_next = jnp.maximum(norm_next, 0.0)
            coef[2 * step + 1] = as_rows(norm_next / norm_now)
            norm_now = norm_next

    images = [outward[step].sums(0) for step in range(2)]
    for ch in range(CHUNKS[3]):
        last = outward[2].sums(ch)
        rows = rows_of(3, ch)
        size = R // CHUNKS[3]
        cut = slice(ch * size, (ch + 1) * size)
        for half in range(2):
            lanes = pl.ds(half * BLOCK, BLOCK)
            residual = direction = right_ref[rows, lanes]
            total = jnp.zeros_like(residual)
            for step in range(3):
                image = last[half] if step == 2 else images[step][half][cut]
                total = total + coef[2 * step, rows, :] * direction
                residual = residual - coef[2 * step, rows, :] * (nugget * direction + image)
                if step < 2:
                    direction = residual + coef[2 * step + 1, rows, :] * direction
            solution_ref[rows, lanes] = total
            residual_ref[rows, lanes] = residual

    assert len(phases) == PHASES
    for phase, view in enumerate(phases):
        pltpu.make_async_copy(view, view, send.at[phase]).wait()


def per_device(side, depth, point_data, right_side, pair_list):
    R = right_side.shape[0]
    chips = side * side
    f32, bf16 = jnp.float32, jnp.bfloat16
    vmem = pl.BlockSpec(memory_space=pltpu.VMEM)
    out = jax.ShapeDtypeStruct(right_side.shape, f32)
    return pl.pallas_call(
        functools.partial(kernel, side, depth),
        out_shape=(out, out),
        in_specs=[pl.BlockSpec(memory_space=pltpu.HBM)] * 2,
        out_specs=(vmem, vmem),
        scratch_shapes=[
            *[pltpu.VMEM((4 * chips + 1, R // n, BLOCK), bf16) for n in CHUNKS for _ in range(n)],
            *[pltpu.VMEM((n, 2 * depth, R // n, BLOCK), bf16) for n in CHUNKS],
            *[pltpu.VMEM((n, 2 * depth, R // n, BLOCK), bf16) for n in CHUNKS],
            pltpu.VMEM((4 * chips + 1, 8, BLOCK), f32),
            pltpu.VMEM((2 * depth, 8, BLOCK), f32),
            pltpu.VMEM((2 * depth, 8, BLOCK), f32),
            pltpu.VMEM((2 * depth, 8, BLOCK), f32),
            pltpu.VMEM((36, 8, BLOCK), f32),
            pltpu.VMEM((3, 36, R, BLOCK), bf16),
            pltpu.VMEM((9, 4 * BLOCK, 2 * BLOCK), bf16),
            pltpu.VMEM((36, R, BLOCK), f32),
            pltpu.VMEM((36, R, BLOCK), f32),
            pltpu.VMEM((3, chips, 4, BLOCK), f32),
            pltpu.VMEM((3, 2 * depth, 4, BLOCK), f32),
            pltpu.VMEM((2, 8, BLOCK), jnp.int32),
            pltpu.SMEM((2, 8, BLOCK), jnp.int32),
            pltpu.VMEM((6, R, BLOCK), f32),
            pltpu.VMEM(point_data.shape, f32),
            pltpu.VMEM(right_side.shape, f32),
            pltpu.SemaphoreType.DMA((PHASES,)),
            pltpu.SemaphoreType.DMA((PHASES,)),
            pltpu.SemaphoreType.DMA((2,)),
        ],
        compiler_params=pltpu.CompilerParams(
            collective_id=0, has_side_effects=True, vmem_limit_bytes=55040 << 10
        ),
    )(point_data, right_side)


def build(mesh, side):
    depth = mesh.shape["row"]
    placed = P(None, ("row", "col"))
    return jax.shard_map(
        functools.partial(per_device, side, depth),
        mesh=mesh,
        in_specs=(placed, placed, P()),
        out_specs=(placed, placed),
        check_vma=False,
    )


def solution(mesh):
    return build(mesh, SIDE)
```

```python
import functools

import jax
import jax.numpy as jnp
from jax import lax
from jax.experimental import pallas as pl
from jax.experimental.pallas import tpu as pltpu
from jax.sharding import PartitionSpec as P

SIDE = 4
BLOCK = 128
MESH = pl.DeviceIdType.MESH
long_range = 1.0
short_range = 0.35
nugget = 1.0
CHUNKS = (4, 1, 1, 4)
PHASES = 14 + 3 * sum(CHUNKS)


def covariance(xj, yj, zj, sj, xi, yi, zi, si):
    dx, dy, dz = xj - xi, yj - yi, zj - zi
    d = jnp.sqrt(dx * dx + dy * dy + dz * dz)

    def wendland(u):
        remain = jnp.maximum(1.0 - u, 0.0)
        square = remain * remain
        return square * square * (4.0 * u + 1.0)

    return sj * (wendland(d * (1.0 / long_range)) + wendland(d * (1.0 / short_range))) * si


def kernel(side, depth, point_hbm, right_hbm, solution_ref, residual_ref, *scratch):
    chips = side * side
    slots = 4 * chips
    zslots = 2 * depth
    R = right_hbm.shape[0]
    g_vec = [list(scratch[sum(CHUNKS[:v]):sum(CHUNKS[:v + 1])]) for v in range(4)]
    zs_vec = scratch[sum(CHUNKS):sum(CHUNKS) + 4]
    zr_vec = scratch[sum(CHUNKS) + 4:sum(CHUNKS) + 8]
    (g_pts, line_pts, zs_pts, zr_pts, h_pts, h_vec, tiles, p_all, r_all, ar_one, ar_two,
     table_v, table_s, coef, point_ref, right_ref, send, recv, local_sem) = scratch[sum(CHUNKS) + 8:]
    my_z = lax.axis_index("row")
    my_col = lax.axis_index("col")
    core = my_col % 2
    chip = my_col // 2
    xx = chip % side
    yy = chip // side
    zs = my_z * 2 + core
    own = (core * chips + chip) * 2
    sibling = (my_z, chip * 2 + 1 - core)

    def rows_of(v, ch):
        size = R // CHUNKS[v]
        return pl.ds(ch * size, size)

    def device(zslot, chip_):
        return (zslot // 2, chip_ * 2 + zslot % 2)

    def shifted(ox, oy):
        return ((yy + oy) % side) * side + (xx + ox) % side

    def plane_peer(o):
        return device(zs, shifted(o % side, o // side))

    def line_peer(o):
        return device((my_z + o) % depth * 2 + core, chip)

    def pillar_peer(o):
        return device((zs + o) % zslots, chip)

    def neighbour(n, oz):
        return device((zs + oz + zslots) % zslots, shifted(n // 3 - 1 + side, n % 3 - 1 + side))

    def push(src, dst, phase, peer):
        pltpu.make_async_remote_copy(
            src_ref=src, dst_ref=dst, send_sem=send.at[phase], recv_sem=recv.at[phase],
            device_id=peer, device_id_type=MESH,
        ).start()

    phases = []

    def new_phase(view):
        phases.append(view)
        return len(phases) - 1

    def arrived(phase):
        view = phases[phase]
        pltpu.make_async_copy(view, view, recv.at[phase]).wait()

    def loop(lo, hi, body):
        lax.fori_loop(lo, hi, lambda i, c: (body(i), c)[1], 0)

    def plane_start(buf, rows=None):
        rows = pl.ds(0, buf.shape[1] if rows is None else rows)
        phase = new_phase(buf.at[pl.ds(0, 2 * (chips - 1)), rows])
        part = buf.at[pl.ds(own, 2), rows]
        loop(1, chips, lambda o: push(part, part, phase, plane_peer(o)))
        return phase

    def forward_start(buf, rows=None):
        rows = pl.ds(0, buf.shape[1] if rows is None else rows)
        phase = new_phase(buf.at[pl.ds(0, 2 * chips), rows])
        part = buf.at[pl.ds(core * 2 * chips, 2 * chips), rows]
        push(part, part, phase, sibling)
        return phase

    def column_start(buf, staged, into, table):
        phase = new_phase(into.at[pl.ds(0, 2 * (depth - 1))])
        for t in range(2 * depth):
            staged[t] = buf[table_s[table, 4, t]]
        into[2 * my_z] = staged[2 * my_z]
        into[2 * my_z + 1] = staged[2 * my_z + 1]

        def one(o):
            z_to = (my_z + o) % depth
            push(staged.at[pl.ds(2 * z_to, 2)], into.at[pl.ds(2 * my_z, 2)], phase, line_peer(o))

        loop(1, depth, one)
        return phase

    def column_sum(into):
        pair = []
        for half in range(2):
            total = into[half].astype(jnp.float32)
            for z in range(1, depth):
                total = total + into[2 * z + half].astype(jnp.float32)
            pair.append(total)
        return pair

    def halo_start(buf):
        phase = new_phase(buf.at[pl.ds(0, 34)])

        def one(n):
            there = (8 - n) * 4

            @pl.when(n != 4)
            def _():
                push(buf.at[pl.ds(17, 2)], buf.at[pl.ds(there + 1, 2)], phase, neighbour(n, 0))

            push(buf.at[pl.ds(18, 1)], buf.at[pl.ds(there, 1)], phase, neighbour(n, 1))
            push(buf.at[pl.ds(17, 1)], buf.at[pl.ds(there + 3, 1)], phase, neighbour(n, -1))

        loop(0, 9, one)
        return phase

    class Journey:
        def __init__(self, v, table):
            self.v, self.table, self.count = v, table, CHUNKS[v]
            self.planes = [plane_start(buf) for buf in g_vec[v]]
            self.forwards, self.columns = [], []

        def forward(self):
            ch = len(self.forwards)
            arrived(self.planes[ch])
            self.forwards.append(forward_start(g_vec[self.v][ch]))

        def column(self):
            ch = len(self.columns)
            arrived(self.forwards[ch])
            self.columns.append(column_start(
                g_vec[self.v][ch], zs_vec[self.v].at[ch], zr_vec[self.v].at[ch], self.table))

        def through(self):
            self.forward()
            for _ in range(1, self.count):
                self.forward()
                self.column()
            self.column()

        def sums(self, ch):
            arrived(self.columns[ch])
            return column_sum(zr_vec[self.v].at[ch])

    load = [
        pltpu.make_async_copy(point_hbm, point_ref, local_sem.at[0]),
        pltpu.make_async_copy(right_hbm, right_ref, local_sem.at[1]),
    ]
    for copy in load:
        copy.start()

    barrier = pltpu.get_barrier_semaphore()

    def greet(peer):
        pl.semaphore_signal(barrier, inc=1, device_id=peer, device_id_type=MESH)

    loop(1, chips, lambda o: greet(plane_peer(o)))
    loop(1, depth, lambda o: greet(line_peer(o)))
    greet(sibling)
    g_pts[:, 5:8, :] = jnp.zeros((slots + 1, 3, BLOCK), jnp.float32)
    load[0].wait()
    pts = point_ref[...]
    for half in range(2):
        here = pts[:, half * BLOCK:(half + 1) * BLOCK]
        low = jnp.broadcast_to(jnp.floor(jnp.min(here, axis=1, keepdims=True)), (4, BLOCK))
        cx = jnp.clip(low[0:1], 0.0, side - 1.0)
        cy = jnp.clip(low[1:2], 0.0, side - 1.0)
        cz = jnp.clip(low[2:3], 0.0, 4.0 * depth - 1.0)
        slab = jnp.floor(cz * 0.25)
        level = cz - 4.0 * slab
        upper = jnp.floor(level * 0.5)
        slot = (upper * chips + cy * side + cx) * 2.0 + (level - 2.0 * upper)
        g_pts[own + half] = jnp.zeros((8, BLOCK), jnp.float32)
        g_pts[own + half, 0:4, :] = here
        g_pts[own + half, 4:5, :] = slab * slots + slot
        g_pts[own + half, 5:6, :] = slot
        g_pts[own + half, 6:7, :] = slab
        line_pts[2 * my_z + half] = g_pts[own + half]
    load[1].wait()
    for half in range(2):
        for ch in range(CHUNKS[0]):
            part = right_ref[rows_of(0, ch), half * BLOCK:(half + 1) * BLOCK]
            g_vec[0][ch][own + half] = part.astype(jnp.bfloat16)
    g_pts[slots] = jnp.zeros((8, BLOCK), jnp.float32)
    for v in range(4):
        for buf in g_vec[v]:
            buf[slots] = jnp.zeros((R // CHUNKS[v], BLOCK), jnp.bfloat16)

    pl.semaphore_wait(barrier, chips - 1 + depth - 1 + 1)

    pts_plane = plane_start(g_pts, 5)
    line = new_phase(line_pts.at[pl.ds(0, 2 * (depth - 1))])
    mine = line_pts.at[pl.ds(2 * my_z, 2)]
    loop(1, depth, lambda o: push(mine, mine, line, line_peer(o)))
    inward = Journey(0, 0)
    arrived(pts_plane)
    pts_forward = forward_start(g_pts, 5)
    arrived(line)

    lane = lax.broadcasted_iota(jnp.int32, (8, BLOCK), 1)
    target = ((lane // 2) * slots + (own + lane % 2)).astype(jnp.float32)
    gap = jnp.float32(slots)
    slab_here = lax.convert_element_type(my_z, jnp.float32)
    acc = jnp.full((8, BLOCK), gap, jnp.float32)
    for t in range(2 * depth):
        tile = line_pts[t]
        value = jnp.where(tile[6:7] == slab_here, tile[5:6], gap)
        acc = jnp.where(lane == t, jnp.broadcast_to(value, (8, BLOCK)), acc)
    table_v[1] = jnp.clip(acc.astype(jnp.int32), 0, slots)

    arrived(pts_forward)
    acc = jnp.full((8, BLOCK), gap, jnp.float32)
    for k in range(slots):
        acc = jnp.minimum(acc, jnp.where(g_pts[k] == target, jnp.float32(k), gap))
    table_v[0] = jnp.clip(acc.astype(jnp.int32), 0, slots)
    copy = pltpu.make_async_copy(table_v, table_s, local_sem.at[0])
    copy.start()
    copy.wait()

    pts_column = column_start(g_pts, zs_pts, zr_pts, 0)
    inward.through()
    arrived(pts_column)
    for half, total in enumerate(column_sum(zr_pts)):
        h_pts[17 + half] = total
    pts_halo = halo_start(h_pts)
    for ch in range(CHUNKS[0]):
        for half, total in enumerate(inward.sums(ch)):
            h_vec[0, 17 + half, rows_of(0, ch), :] = total.astype(jnp.bfloat16)
    halo = halo_start(h_vec.at[0])

    arrived(pts_halo)

    def tile_column(n):
        for level in range(4):
            other = jnp.transpose(h_pts[n * 4 + level])
            xj, yj, zj, sj = (other[:, a:a + 1] for a in range(4))
            for half in range(2):
                rows, lanes = pl.ds(level * BLOCK, BLOCK), pl.ds(half * BLOCK, BLOCK)
                if not 0 <= level - half <= 2:
                    tiles[n, rows, lanes] = jnp.zeros((BLOCK, BLOCK), jnp.bfloat16)
                    continue
                xi, yi, zi, si = (h_pts[17 + half, a:a + 1, :] for a in range(4))
                tiles[n, rows, lanes] = covariance(xj, yj, zj, sj, xi, yi, zi, si).astype(jnp.bfloat16)

    loop(0, 9, tile_column)

    eye = lax.broadcasted_iota(jnp.int32, (R, BLOCK), 0) == lax.broadcasted_iota(jnp.int32, (R, BLOCK), 1)
    row4 = lax.broadcasted_iota(jnp.int32, (4, BLOCK), 0)

    def as_lanes(values):
        total = jnp.sum(values, axis=1, keepdims=True)
        return jnp.sum(jnp.where(eye, total, 0.0), axis=0, keepdims=True)

    def as_rows(values):
        column = jnp.sum(jnp.where(eye, values, 0.0), axis=1, keepdims=True)
        return jnp.broadcast_to(column, (R, BLOCK))

    def sum_start(step, rows):
        tile = jnp.zeros((4, BLOCK), jnp.float32)
        for i, value in enumerate(rows):
            tile = jnp.where(row4 == i, value, tile)
        buf = ar_one.at[step]
        buf[chip] = tile
        phase = new_phase(buf.at[pl.ds(0, chips - 1)])
        part = buf.at[pl.ds(chip, 1)]
        loop(1, chips, lambda o: push(part, part, phase, plane_peer(o)))
        return phase

    def sum_second(step, phase):
        arrived(phase)
        buf, second = ar_one.at[step], ar_two.at[step]
        total = buf[0]
        for i in range(1, chips):
            total = total + buf[i]
        second[zs] = total
        phase = new_phase(second.at[pl.ds(0, zslots - 1)])
        part = second.at[pl.ds(zs, 1)]
        loop(1, zslots, lambda o: push(part, part, phase, pillar_peer(o)))
        return phase

    def sum_finish(step, phase):
        arrived(phase)
        second = ar_two.at[step]
        total = second[0]
        for i in range(1, zslots):
            total = total + second[i]
        return total

    outward = []
    norm_now = None
    for step in range(3):
        arrived(halo)
        product = jnp.zeros((R, 2 * BLOCK), jnp.float32)
        for n in range(9):
            parts = []
            for level in range(4):
                k = n * 4 + level
                if step == 0:
                    parts.append(h_vec[0, k])
                    continue
                if step == 1:
                    p_old = h_vec[0, k].astype(jnp.float32)
                    r_old = p_old
                else:
                    p_old, r_old = p_all[k], r_all[k]
                image = nugget * p_old + h_vec[step, k].astype(jnp.float32)
                r_new = r_old - coef[2 * step - 2] * image
                p_new = r_new + coef[2 * step - 1] * p_old
                r_all[k] = r_new
                p_all[k] = p_new
                parts.append(p_new.astype(jnp.bfloat16))
            lhs = jnp.concatenate(parts, axis=1)
            product = product + jnp.dot(lhs, tiles[n], preferred_element_type=jnp.float32)
        pq = rq = qq = rr = jnp.zeros((R, BLOCK), jnp.float32)
        for half in range(2):
            if step == 0:
                p_own = h_vec[0, 17 + half].astype(jnp.float32)
                r_own = p_own
            else:
                p_own, r_own = p_all[17 + half], r_all[17 + half]
            rounded = product[:, half * BLOCK:(half + 1) * BLOCK].astype(jnp.bfloat16)
            if step < 2:
                h_vec[step + 1, 17 + half] = rounded
            for ch in range(CHUNKS[step + 1]):
                size = R // CHUNKS[step + 1]
                g_vec[step + 1][ch][own + half] = rounded[ch * size:(ch + 1) * size]
            q = nugget * p_own + rounded.astype(jnp.float32)
            pq, rq, qq = pq + p_own * q, rq + r_own * q, qq + q * q
            rr = rr + r_own * r_own
        rows = [as_lanes(a) for a in ((pq, rq, qq, rr) if step == 0 else (pq, rq, qq))]
        ar = sum_start(step, rows)
        if step < 2:
            halo = halo_start(h_vec.at[step + 1])
        if step == 2:
            outward.append(Journey(3, 1))
        if step > 0:
            outward[step - 1].forward()
        ar = sum_second(step, ar)
        if step > 0:
            outward[step - 1].column()
        if step < 2:
            outward.append(Journey(step + 1, 1))
        else:
            outward[2].through()
        totals = sum_finish(step, ar)
        if step == 0:
            norm_now = totals[3:4]
        alpha = norm_now / totals[0:1]
        coef[2 * step] = as_rows(alpha)
        if step < 2:
            norm_next = norm_now - 2.0 * alpha * totals[1:2] + alpha * alpha * totals[2:3]
            norm_next = jnp.maximum(norm_next, 0.0)
            coef[2 * step + 1] = as_rows(norm_next / norm_now)
            norm_now = norm_next

    images = [outward[step].sums(0) for step in range(2)]
    for ch in range(CHUNKS[3]):
        last = outward[2].sums(ch)
        rows = rows_of(3, ch)
        size = R // CHUNKS[3]
        cut = slice(ch * size, (ch + 1) * size)
        for half in range(2):
            lanes = pl.ds(half * BLOCK, BLOCK)
            residual = direction = right_ref[rows, lanes]
            total = jnp.zeros_like(residual)
            for step in range(3):
                image = last[half] if step == 2 else images[step][half][cut]
                total = total + coef[2 * step, rows, :] * direction
                residual = residual - coef[2 * step, rows, :] * (nugget * direction + image)
                if step < 2:
                    direction = residual + coef[2 * step + 1, rows, :] * direction
            solution_ref[rows, lanes] = total
            residual_ref[rows, lanes] = residual

    assert len(phases) == PHASES
    for phase, view in enumerate(phases):
        pltpu.make_async_copy(view, view, send.at[phase]).wait()


def per_device(side, depth, point_data, right_side, pair_list):
    R = right_side.shape[0]
    chips = side * side
    f32, bf16 = jnp.float32, jnp.bfloat16
    vmem = pl.BlockSpec(memory_space=pltpu.VMEM)
    out = jax.ShapeDtypeStruct(right_side.shape, f32)
    return pl.pallas_call(
        functools.partial(kernel, side, depth),
        out_shape=(out, out),
        in_specs=[pl.BlockSpec(memory_space=pltpu.HBM)] * 2,
        out_specs=(vmem, vmem),
        scratch_shapes=[
            *[pltpu.VMEM((4 * chips + 1, R // n, BLOCK), bf16) for n in CHUNKS for _ in range(n)],
            *[pltpu.VMEM((n, 2 * depth, R // n, BLOCK), bf16) for n in CHUNKS],
            *[pltpu.VMEM((n, 2 * depth, R // n, BLOCK), bf16) for n in CHUNKS],
            pltpu.VMEM((4 * chips + 1, 8, BLOCK), f32),
            pltpu.VMEM((2 * depth, 8, BLOCK), f32),
            pltpu.VMEM((2 * depth, 8, BLOCK), f32),
            pltpu.VMEM((2 * depth, 8, BLOCK), f32),
            pltpu.VMEM((36, 8, BLOCK), f32),
            pltpu.VMEM((3, 36, R, BLOCK), bf16),
            pltpu.VMEM((9, 4 * BLOCK, 2 * BLOCK), bf16),
            pltpu.VMEM((36, R, BLOCK), f32),
            pltpu.VMEM((36, R, BLOCK), f32),
            pltpu.VMEM((3, chips, 4, BLOCK), f32),
            pltpu.VMEM((3, 2 * depth, 4, BLOCK), f32),
            pltpu.VMEM((2, 8, BLOCK), jnp.int32),
            pltpu.SMEM((2, 8, BLOCK), jnp.int32),
            pltpu.VMEM((6, R, BLOCK), f32),
            pltpu.VMEM(point_data.shape, f32),
            pltpu.VMEM(right_side.shape, f32),
            pltpu.SemaphoreType.DMA((PHASES,)),
            pltpu.SemaphoreType.DMA((PHASES,)),
            pltpu.SemaphoreType.DMA((2,)),
        ],
        compiler_params=pltpu.CompilerParams(
            collective_id=0, has_side_effects=True, vmem_limit_bytes=55040 << 10
        ),
    )(point_data, right_side)


def build(mesh, side):
    depth = mesh.shape["row"]
    placed = P(None, ("row", "col"))
    return jax.shard_map(
        functools.partial(per_device, side, depth),
        mesh=mesh,
        in_specs=(placed, placed, P()),
        out_specs=(placed, placed),
        check_vma=False,
    )


def solution(mesh):
    return build(mesh, SIDE)
```
